32 devices in a mesh: groups: 2 (over x), dev: 8 (over z, y), sub: 2 (over core).
Axes of the slice: x: 2, y: 2, z: 4, core: 2. Of those that a mesh axis runs over, the one named last changes fastest.
Arguments:
- hidden: bfloat16 [128, 6144], P(('groups', 'dev')), parts along dimension 0, may hold values from -6 to 6
- query: bfloat16 [128, 48, 128], P(('groups', 'dev'), 'sub'), parts along dimension 0, may hold values from -180 to 180
- cache_keys: bfloat16 [128, 8, 64, 128], P(('groups', 'dev'), 'sub'), parts along dimension 0, may hold values from -6 to 6
- cache_values: bfloat16 [128, 8, 64, 128], P(('groups', 'dev'), 'sub'), parts along dimension 0, may hold values from -6 to 6
- lengths: int32 [128], P(('groups', 'dev')), parts along dimension 0, may hold values from 16 to 64
- out_proj: bfloat16 [6144, 6144], P('sub', 'dev'), may hold values from -0.078125 to 0.078125
- norm_gain: float32 [6144], replicated, may hold values from 0.1 to 1.9
- router: bfloat16 [6144, 4], replicated, may hold values from -0.078125 to 0.078125
- low_factor: bfloat16 [6144, 256], P('sub'), may hold values from -0.078125 to 0.078125
- gate_weight: bfloat16 [6144, 32768], P(None, ('dev', 'sub')), may hold values from -0.078125 to 0.078125
- up_weight: bfloat16 [6144, 32768], P(None, ('dev', 'sub')), may hold values from -0.078125 to 0.078125
- down_weight: bfloat16 [32768, 6144], P(('dev', 'sub')), may hold values from -0.0625 to 0.0625
- gate_low: bfloat16 [256, 32768], P(None, ('dev', 'sub')), may hold values from -0.375 to 0.375
- up_low: bfloat16 [256, 32768], P(None, ('dev', 'sub')), may hold values from -0.375 to 0.375
- experts: int32 [128, 2], P(('groups', 'dev')), parts along dimension 0, may hold values from 0 to 3, all different within a row; in each aligned block of 8 rows (0 to 7, 8 to 15, ...) at most 6 rows name the same one
Outputs:
- layer_out: bfloat16 [128, 6144], P(('groups', 'dev')), parts along dimension 0
- mixture: float32 [128, 6144], P(('groups', 'dev')), parts along dimension 0
The draws below stay inside these ranges and needn't reach their ends.
There are 2 independent parts, one for each index of `groups`. The reference program is written for one: setup_inputs(seed, part) draws one part's arguments, and reference() takes and returns one part's arrays. A program takes and returns all parts, laid end to end along the dimension named above; an argument that names none is the same for every part. Nothing has to cross between parts.
Inputs may be any that keep to these rules, and one draw needn't show every extreme that they name: Each row names two different experts. Among the 8 requests of one device no expert is named more than 6 times, and that bound is reached on some device.
All inputs are finite; a program needn't handle non-finite values.
Results may differ from the reference program's by a relative error of at most 0.015.
Values may be sent and summed in bfloat16 or wider, within the bound.
No kernel may reach another device: no remote copies, remote signals or barrier semaphores. Data moves between devices by JAX's collectives and lax.ppermute only.
A program may use at most 128 MiB of HBM per device.

```python
import math
import jax
import jax.numpy as jnp
import numpy as np
from jax import lax

D = 6144
QH = 48
KVH = 8
HD = 128
EXPERTS = 4
FF = 8192
RANK = 256
REQ_DEV = 8
SPAN = 64
CAP = 6
REQ = 64


def drawn_pair(key):
    streams = jax.random.split(jax.random.fold_in(key, 31), 2)
    query_draw = jnp.clip(jax.random.normal(streams[0], (REQ, QH, HD), jnp.float32), -6.0, 6.0)
    key_draw = jnp.clip(jax.random.normal(streams[1], (REQ, KVH, SPAN, HD), jnp.float32), -6.0, 6.0)
    return (query_draw, key_draw)


def draw_query(key, part):
    return drawn_pair(key)[0].astype(jnp.bfloat16)


def draw_cache_keys(key, part):
    return drawn_pair(key)[1].astype(jnp.bfloat16)


def set_ends(array, key, least, high):
    spot = [jax.random.randint(jax.random.fold_in(key, axis), (), 0, length) for axis, length in enumerate(array.shape)]
    main_axis = array.shape.index(max(array.shape))
    next_to = spot[:main_axis] + [(spot[main_axis] + 1) % array.shape[main_axis]] + spot[main_axis + 1:]
    return array.at[tuple(spot)].set(least).at[tuple(next_to)].set(high)


def levels(rng, shape, cuts, smallest, top_value):
    def one(axis_at, shards_of):
        draws = jax.random.uniform(jax.random.fold_in(jax.random.fold_in(rng, 6), axis_at), (shards_of,), jnp.float32, smallest / len(cuts), top_value / len(cuts))
        return jnp.repeat(jnp.exp(draws), shape[axis_at] // shards_of).reshape((-1,) + (1,) * (len(shape) - axis_at - 1))

    loudness = one(*cuts[0])
    for cut in cuts[1:]:
        loudness = loudness * one(*cut)
    return loudness


def assign_block(key, own, number, rows, amount, top, most, slope):
    sequence = jax.random.permutation(key, amount)
    heavy_load, usual = portions_of(amount, rows * top, most, slope, True), portions_of(amount, rows * top, most, slope, False)
    places = jnp.arange(amount)

    def named(sizes, offset_by):
        used = int((sizes > 0).sum())
        fixed = max(1, used // 4)
        shifted = fixed + (places - fixed + offset_by * (used - fixed)) % max(1, amount - fixed)
        return jnp.zeros((amount,), jnp.int32).at[sequence[jnp.where(places < fixed, places, shifted)]].set(jnp.asarray(sizes, jnp.int32))

    sizes = jnp.where(number % 4 == 0, named(heavy_load, number // 4), named(usual, number - number // 4 - 1))
    mixed = jax.random.permutation(jax.random.fold_in(own, 3), amount)
    source_of, sink = mixed[0:amount // 2 * 2:2], mixed[1:amount // 2 * 2:2]
    room = jnp.minimum(sizes[source_of] - 1, most - sizes[sink]) // 2
    room = jnp.where((source_of == sequence[0]) | (sink == sequence[0]) | (sizes[sink] == 0), 0, jnp.maximum(room, 0))
    shifted = jax.random.randint(jax.random.fold_in(own, 4), (amount // 2,), 0, 1 << 20) % (room + 1)
    sizes = sizes.at[source_of].add(-shifted).at[sink].add(shifted)
    items = jnp.searchsorted(jnp.cumsum(sizes), jnp.arange(rows * top), side="right").astype(jnp.int32)
    table = items.reshape(top, rows).T
    table = table[jax.random.permutation(jax.random.fold_in(own, 1), rows)]
    offset_by = jax.random.randint(jax.random.fold_in(own, 2), (rows, 1), 0, top)
    return jnp.take_along_axis(table, (jnp.arange(top)[None, :] + offset_by) % top, axis=1)


def portions_of(count, total, limit, skew, full):
    portions = [(1 << 20) // math.isqrt(rank ** skew) + 1 for rank in range(1, count + 1)]
    largest = limit if full else min(limit, max(-(-total // count), total * portions[0] // sum(portions)))
    least = 1 if total - largest >= count - 1 else 0
    holding, surplus = [largest] + [least] * (count - 1), total - largest - least * (count - 1)
    while surplus > 0:
        free = [i for i in range(1, count) if holding[i] < largest] or [i for i in range(1, count) if holding[i] < limit]
        pool, budget = sum([portions[i] for i in free]), surplus
        for i in free:
            extra = min(limit - holding[i], max(1, budget * portions[i] // pool), surplus)
            holding[i] = holding[i] + extra
            surplus = surplus - extra
    return np.array(holding)


def scatter_about(rng, shape, scale, reach, cuts=(), kind=jnp.bfloat16):
    array = jax.random.normal(rng, shape, jnp.float32) * scale
    if len(cuts) > 0:
        array = levels(rng, shape, cuts, -0.22, 0.18) * array
    return jnp.clip(array, min=-reach, max=reach).astype(kind)


def setup_inputs(seed: int = 0, part: int = 0) -> dict:
    arg_keys = jax.random.split(jax.random.key(seed), 16)
    part_keys = jax.random.split(jax.random.fold_in(arg_keys[15], part), 16)
    hidden = scatter_about(part_keys[0], (REQ, D), 1.0, 6.0, ((0, 8),))
    query = draw_query(jax.random.fold_in(jax.random.fold_in(arg_keys[15], part), 71), part)
    cache_keys = draw_cache_keys(jax.random.fold_in(jax.random.fold_in(arg_keys[15], part), 71), part)
    cache_values = scatter_about(part_keys[3], (REQ, KVH, SPAN, HD), 1.0, 6.0, ((0, 8), (1, 2)))
    lengths = set_ends(jax.random.randint(part_keys[4], (REQ,), SPAN // 4, SPAN + 1), jax.random.fold_in(part_keys[4], 1), SPAN // 4, SPAN).astype(jnp.int32)
    out_proj = scatter_about(arg_keys[5], (QH * HD, D), (QH * HD) ** -0.5, 0.078125, ((0, 2), (1, 8)))
    norm_gain = jnp.clip(1.0 + 0.18 * jax.random.normal(arg_keys[6], (D,), jnp.float32), 0.1, 1.9)
    router = scatter_about(arg_keys[7], (D, EXPERTS), D ** -0.5, 0.078125)
    low_factor = scatter_about(arg_keys[8], (D, RANK), D ** -0.5, 0.078125, ((0, 2),))
    gate_weight = scatter_about(arg_keys[9], (D, EXPERTS * FF), D ** -0.5, 0.078125, ((1, 16),))
    up_weight = scatter_about(arg_keys[10], (D, EXPERTS * FF), D ** -0.5, 0.078125, ((1, 16),))
    down_weight = scatter_about(arg_keys[11], (EXPERTS * FF, D), FF ** -0.5, 0.0625, ((0, 16),))
    gate_low = scatter_about(arg_keys[12], (RANK, EXPERTS * FF), RANK ** -0.5, 0.375, ((1, 16),))
    up_low = scatter_about(arg_keys[13], (RANK, EXPERTS * FF), RANK ** -0.5, 0.375, ((1, 16),))
    experts_keys = jax.random.split(jax.random.fold_in(part_keys[14], 1), REQ // REQ_DEV)
    experts_turns = jax.random.permutation(jax.random.fold_in(part_keys[14], 3), REQ // REQ_DEV)
    experts = jax.vmap(lambda own, number: assign_block(jax.random.fold_in(part_keys[14], 2), own, number, REQ_DEV, EXPERTS, 2, CAP, 2))(experts_keys, experts_turns).reshape((REQ, 2))
    return dict(hidden=hidden, query=query, cache_keys=cache_keys, cache_values=cache_values, lengths=lengths, out_proj=out_proj, norm_gain=norm_gain, router=router, low_factor=low_factor, gate_weight=gate_weight, up_weight=up_weight, down_weight=down_weight, gate_low=gate_low, up_low=up_low, experts=experts)


EPSILON = 1e-05

def expert_shard(row_block, low_rank, gate_weight, up_weight, down_weight, gate_low, up_low):
    gate_sum = jnp.dot(row_block, gate_weight, preferred_element_type=jnp.float32) + jnp.dot(low_rank, gate_low, preferred_element_type=jnp.float32)
    up_sum = jnp.dot(row_block, up_weight, preferred_element_type=jnp.float32) + jnp.dot(low_rank, up_low, preferred_element_type=jnp.float32)
    inner_act = (jax.nn.silu(gate_sum) * up_sum).astype(jnp.bfloat16)
    return jnp.dot(inner_act, down_weight, preferred_element_type=jnp.float32)

def route_gates(normed, router, experts):
    logits = jnp.dot(normed, router, preferred_element_type=jnp.float32)
    labels = lax.broadcasted_iota(jnp.int32, (1, 1, router.shape[1]), 2)
    picked = (experts[:, :, None] == labels).astype(jnp.float32)
    chosen = lax.optimization_barrier(jnp.sum(logits[:, None, :] * picked, axis=-1))
    leading = jax.nn.sigmoid(chosen[:, 0] - chosen[:, 1])
    return jnp.stack([leading, 1.0 - leading], axis=-1)

def reference(hidden, query, cache_keys, cache_values, lengths, out_proj, norm_gain, router, low_factor, gate_weight, up_weight, down_weight, gate_low, up_low, experts):
    heads_per_kv = QH // KVH
    grouped = query.astype(jnp.float32).reshape(REQ, KVH, heads_per_kv, HD)
    scores = jnp.einsum('rkgd,rkld->rkgl', grouped, cache_keys.astype(jnp.float32)) * HD ** (-0.5)
    visible = lax.broadcasted_iota(jnp.int32, (REQ, SPAN), 1) < lengths[:, None]
    scores = jnp.where(visible[:, None, None, :], scores, -1e+30)
    attn_probs = jax.nn.softmax(scores, axis=-1).astype(jnp.bfloat16)
    attended = jnp.einsum('rkgl,rkld->rkgd', attn_probs.astype(jnp.float32), cache_values.astype(jnp.float32))
    attended = attended.astype(jnp.bfloat16).reshape(REQ, QH * HD)
    residual = hidden.astype(jnp.float32) + jnp.dot(attended, out_proj, preferred_element_type=jnp.float32)
    inverse = lax.rsqrt(lax.optimization_barrier(jnp.mean(residual * residual, axis=-1, keepdims=True)) + EPSILON)
    normed = (residual * inverse * norm_gain).astype(jnp.bfloat16)
    low_rank = jnp.dot(normed, low_factor, preferred_element_type=jnp.float32).astype(jnp.bfloat16)
    gate_pair = route_gates(normed, router, experts)
    mixture = jnp.zeros((REQ, D), jnp.float32)
    for expert in range(EXPERTS):
        columns = slice(expert * FF, (expert + 1) * FF)
        output = expert_shard(normed, low_rank, gate_weight[:, columns], up_weight[:, columns], down_weight[columns, :], gate_low[:, columns], up_low[:, columns])
        route_share = lax.optimization_barrier(jnp.sum(gate_pair * (experts == expert).astype(jnp.float32), axis=-1))
        mixture = mixture + route_share[:, None] * output
    return ((residual + mixture).astype(jnp.bfloat16), mixture)
```

```python
import functools

import jax
import jax.numpy as jnp
from jax import lax
from jax.experimental import pallas as pl
from jax.experimental.pallas import tpu as pltpu
from jax.sharding import PartitionSpec as P

CAP = 6
EPSILON = 1e-05
READY = (2, 1, 1, 1, 1)
MIB = 1 << 20
LANES = 128


def vmem():
    return pl.BlockSpec(memory_space=pltpu.VMEM)


def hbm():
    return pl.BlockSpec(memory_space=pltpu.HBM)


def in_hbm(value):
    return pltpu.with_memory_space_constraint(value, pltpu.HBM)


def params(limit_mib):
    return pltpu.CompilerParams(vmem_limit_bytes=limit_mib * MIB)


def cost(flops, bytes_accessed):
    return pl.CostEstimate(flops=int(flops), bytes_accessed=int(bytes_accessed), transcendentals=0)


def attention_kernel(
    dev_count, lengths_hbm, query_hbm, keys_hbm, values_hbm, hidden_hbm, *refs
):
    out_refs = refs[:dev_count]
    lengths_ref, query_ref, keys_ref, values_ref, hidden_ref, rows_ref, sems = refs[dev_count:]
    me, sub = lax.axis_index("dev"), lax.axis_index("sub")
    requests, heads, head_size = query_ref.shape
    kv_heads, span = keys_ref.shape[1], keys_ref.shape[2]
    group = heads // kv_heads
    slots = kv_heads * span
    copies = [
        pltpu.make_async_copy(source, target, sems.at[number])
        for number, (source, target) in enumerate(
            (
                (lengths_hbm, lengths_ref),
                (query_hbm, query_ref),
                (keys_hbm, keys_ref),
                (values_hbm, values_ref),
                (hidden_hbm, hidden_ref),
            )
        )
    ]
    for copy in copies:
        copy.start()
    column = lax.broadcasted_iota(jnp.int32, (heads, slots), 1)
    owner = lax.broadcasted_iota(jnp.int32, (heads, slots), 0) // group
    position = column - owner * span
    for copy in copies[:3]:
        copy.wait()
    scores = [
        lax.dot_general(
            query_ref[r],
            keys_ref[r].reshape(slots, head_size),
            (((1,), (1,)), ((), ())),
            preferred_element_type=jnp.float32,
        )
        for r in range(requests)
    ]
    probs = []
    for r in range(requests):
        visible = (position >= 0) & (position < jnp.minimum(lengths_ref[r], span))
        score = jnp.where(visible, scores[r] * head_size ** (-0.5), -1e30)
        weight = jnp.exp(score - jnp.max(score, axis=1, keepdims=True))
        probs.append((weight / jnp.sum(weight, axis=1, keepdims=True)).astype(jnp.bfloat16))
    copies[3].wait()
    for r in range(requests):
        rows_ref[r] = jnp.dot(
            probs[r], values_ref[r].reshape(slots, head_size), preferred_element_type=jnp.float32
        )
    for h in range(heads):
        value = rows_ref[:, h, :].astype(jnp.bfloat16)
        for out_ref in out_refs:
            out_ref[:, h * head_size : (h + 1) * head_size] = value
    half = hidden_ref.shape[1] // (2 * dev_count)
    copies[4].wait()
    for step in range(dev_count):
        at = pl.multiple_of(((me ^ step) * 2 + sub) * half, LANES)
        out_refs[step][:, heads * head_size :] = hidden_ref[:, pl.ds(at, half)]


def half_block(piece, width):
    sub = lax.axis_index("sub")
    side = sub if piece[1] else 1 - sub
    return pl.multiple_of(((lax.axis_index("dev") ^ piece[0]) * 2 + side) * width, LANES)


class Weights:
    def __init__(self, pieces, width, sources, buffers, sems):
        self.pieces, self.width, self.sources, self.buffers, self.sems = pieces, width, sources, buffers, sems

    def _factor(self, index, source):
        base = half_block(self.pieces[index], self.width)
        rows = source.shape[0]
        at = pl.multiple_of(jnp.where(base >= rows, base - rows, base), LANES)
        return pltpu.make_async_copy(
            source.at[pl.ds(at, self.width), :], self.buffers[2].at[index], self.sems.at[index, 2]
        )

    def _plain(self, index):
        at = pl.ds(half_block(self.pieces[index], self.width), self.width)
        return [
            pltpu.make_async_copy(self.sources[k].at[at, :], self.buffers[k].at[index], self.sems.at[index, k])
            for k in range(2)
        ]

    def start(self, index):
        if index >= len(self.pieces):
            return
        mine, theirs = self.sources[2:]
        base = half_block(self.pieces[index], self.width)
        here = (base >= mine.shape[0]) == (lax.axis_index("sub") == 1)
        for copy in self._plain(index):
            copy.start()

        @pl.when(here)
        def _():
            self._factor(index, mine).start()

        @pl.when(jnp.logical_not(here))
        def _():
            self._factor(index, theirs).start()

    def wait(self, index):
        for copy in self._plain(index):
            copy.wait()
        self._factor(index, self.sources[2]).wait()


def prefetch_kernel(pieces, after_ref, *refs):
    sources, refs = refs[:4], refs[4:]
    plain = (len(refs) - 5) // 2
    plain_sources, refs = refs[:plain], refs[plain:]
    buffers, plain_buffers = refs[:3], refs[3 : 3 + plain]
    sems, plain_sems = refs[3 + plain :]
    weights = Weights(pieces, buffers[0].shape[1], sources, buffers, sems)
    copies = [
        pltpu.make_async_copy(source, target, plain_sems.at[number])
        for number, (source, target) in enumerate(zip(plain_sources, plain_buffers))
    ]
    for copy in copies:
        copy.start()
    for index in range(len(pieces)):
        weights.start(index)
    for copy in copies:
        copy.wait()
    for index in range(len(pieces)):
        weights.wait(index)


def projection_kernel(dev_count, weight_ref, *refs):
    got_refs, (out_ref, stacked) = refs[:dev_count], refs[dev_count:]
    me, sub = lax.axis_index("dev"), lax.axis_index("sub")
    own_rows = got_refs[0].shape[0]
    depth = weight_ref.shape[0]
    half = got_refs[0].shape[1] - depth
    for step in range(dev_count):
        stacked[step * own_rows : (step + 1) * own_rows, :] = got_refs[step][:, :depth]
    product = jnp.dot(stacked[...], weight_ref[...], preferred_element_type=jnp.float32)
    columns = pl.ds(pl.multiple_of(sub * half, LANES), half)
    for step in range(dev_count):
        rows = pl.ds(pl.multiple_of((me ^ step) * own_rows, own_rows), own_rows)
        out_ref[rows, :] = product[step * own_rows : (step + 1) * own_rows, :]
        out_ref[rows, columns] = out_ref[rows, columns] + got_refs[step][:, depth:].astype(jnp.float32)


def residual_kernel(mine_ref, other_ref, full_ref, half_ref, sums):
    sub = lax.axis_index("sub")
    half = half_ref.shape[1]
    sums[...] = mine_ref[...] + other_ref[...]
    full_ref[...] = sums[...].astype(jnp.bfloat16)
    half_ref[...] = sums[:, pl.ds(pl.multiple_of(sub * half, LANES), half)].astype(jnp.bfloat16)


def expert_in_kernel(plan, ready, first, last, *refs):
    refs = list(refs)

    def take(count):
        taken, refs[:] = refs[:count], refs[count:]
        return taken

    operands = 1 + max(piece[0] for piece in plan)
    sources, held = take(4), take(3)
    router_ref, gain_ref = take(2)
    x_refs = take(operands)
    before = None if first else take(4)
    if last:
        experts_ref, gate_low_ref, up_low_ref = take(3)
        inner_ref, share_ref, resid_ref = take(3)
        gate_sum, up_sum, small, names, names_sem = take(5)
        names_copy = pltpu.make_async_copy(experts_ref, names, names_sem)
        names_copy.start()
    else:
        gate_sum, up_sum, small, resid_ref = take(4)
    pieces = [piece[2] for piece in plan]
    width = held[0].shape[1]
    weights = None
    if len(ready) < len(plan):
        buffers, (sems,) = take(3), take(1)
        weights = Weights(pieces[len(ready) :], width, sources, buffers, sems)
        for index in range(3):
            weights.start(index)
    me, sub = lax.axis_index("dev"), lax.axis_index("sub")
    rank, experts = held[2].shape[2], router_ref.shape[0]
    own_rows, model_width = resid_ref.shape
    if first:
        gate_sum[...] = jnp.zeros_like(gate_sum)
        up_sum[...] = jnp.zeros_like(up_sum)
        small[...] = jnp.zeros_like(small)
    else:
        for now, earlier in zip((gate_sum, up_sum, small, resid_ref), before):
            now[...] = earlier[...]
    my_rows = pl.ds(pl.multiple_of(me * own_rows, own_rows), own_rows)
    for index, (operand, which, piece) in enumerate(plan):
        base = half_block(piece, width)
        if which is None:
            side = sub if piece[1] else 1 - sub
            source, columns = x_refs[operand], pl.ds(pl.multiple_of(side * width, LANES), width)
        else:
            source, columns = x_refs[operand].at[which], slice(0, width)
        x = source[:, columns].astype(jnp.float32)
        small[:, rank + LANES :] += jnp.sum(x * x, axis=1, keepdims=True)
        resid_ref[:, pl.ds(base, width)] = source[my_rows, columns]
        x = (x * gain_ref[:, pl.ds(base, width)]).astype(jnp.bfloat16)
        small[:, rank : rank + experts] += lax.dot_general(
            x, router_ref[:, pl.ds(base, width)], (((1,), (1,)), ((), ())), preferred_element_type=jnp.float32
        )
        if index < len(ready):
            blocks = [ref.at[ready[index]] for ref in held]
        else:
            slot = index - len(ready)
            weights.wait(slot)
            weights.start(slot + 3)
            blocks = [ref.at[slot] for ref in buffers]
        gate_sum[...] += jnp.dot(x, blocks[0][...], preferred_element_type=jnp.float32)
        up_sum[...] += jnp.dot(x, blocks[1][...], preferred_element_type=jnp.float32)
        small[:, :rank] += jnp.dot(x, blocks[2][...], preferred_element_type=jnp.float32)
    if not last:
        return
    inverse = lax.rsqrt(small[:, rank + LANES : rank + LANES + 1] / model_width + EPSILON)
    low_rank = (small[:, :rank] * inverse).astype(jnp.bfloat16)
    gate = gate_sum[...] * inverse + jnp.dot(
        low_rank, gate_low_ref[...], preferred_element_type=jnp.float32
    )
    up = up_sum[...] * inverse + jnp.dot(
        low_rank, up_low_ref[...], preferred_element_type=jnp.float32
    )
    inner_ref[...] = (jax.nn.silu(gate) * up).astype(jnp.bfloat16)
    mine = small[my_rows, :]
    inverse = lax.rsqrt(mine[:, rank + LANES : rank + LANES + 1] / model_width + EPSILON)
    logits = mine[:, rank : rank + LANES] * inverse
    lanes = lax.broadcasted_iota(jnp.int32, (own_rows, LANES), 1)
    numbers = lax.broadcasted_iota(jnp.int32, (own_rows, LANES), 0)
    one, two = jnp.zeros_like(numbers), jnp.zeros_like(numbers)
    names_copy.wait()
    for r in range(own_rows):
        one = jnp.where(numbers == r, names[0, r], one)
        two = jnp.where(numbers == r, names[1, r], two)
    chosen_one = jnp.sum(jnp.where(lanes == one, logits, 0.0), axis=1, keepdims=True)
    chosen_two = jnp.sum(jnp.where(lanes == two, logits, 0.0), axis=1, keepdims=True)
    leading = jax.nn.sigmoid(chosen_one - chosen_two)
    share_ref[...] = jnp.where(lanes == one, leading, 0.0) + jnp.where(lanes == two, 1.0 - leading, 0.0)


def expert_out_kernel(own, down_ref, inner_ref, out_ref, buf, sems):
    sub = lax.axis_index("sub")
    blocks, _, block = buf.shape
    side = sub if own else 1 - sub

    def copy(index):
        start = pl.multiple_of((side * blocks + index) * block, LANES)
        return pltpu.make_async_copy(down_ref.at[:, pl.ds(start, block)], buf.at[index], sems.at[index])

    for index in range(min(3, blocks)):
        copy(index).start()
    for index in range(blocks):
        copy(index).wait()
        if index + 3 < blocks:
            copy(index + 3).start()
        product = jnp.dot(inner_ref[...], buf[index], preferred_element_type=jnp.float32)
        out_ref[:, index * block : (index + 1) * block] = product.astype(out_ref.dtype)


def split_kernel(dev_count, mine_ref, other_ref, *out_refs):
    me = lax.axis_index("dev")
    rows = out_refs[0].shape[0]
    for step in range(dev_count):
        at = pl.ds(pl.multiple_of((me ^ step) * rows, rows), rows)
        out_refs[step][...] = (mine_ref[at, :] + other_ref[at, :].astype(jnp.float32)).astype(jnp.bfloat16)


def mixture_kernel(holders, share_ref, *refs):
    part_refs, out_ref = refs[:-1], refs[-1]
    me = lax.axis_index("dev")
    lanes = lax.broadcasted_iota(jnp.int32, share_ref.shape, 1)
    total = jnp.zeros(out_ref.shape, jnp.float32)
    for step, ref in enumerate(part_refs):
        expert = (me ^ step) // holders
        share = jnp.sum(jnp.where(lanes == expert, share_ref[...], 0.0), axis=1, keepdims=True)
        total = total + ref[...].astype(jnp.float32) * share
    out_ref[...] = total.astype(jnp.bfloat16)


def output_kernel(mine_ref, other_ref, resid_ref, layer_ref, mixture_ref):
    sub = lax.axis_index("sub")
    half = mine_ref.shape[1]
    for ref, side in ((mine_ref, sub), (other_ref, 1 - sub)):
        at = pl.ds(pl.multiple_of(side * half, LANES), half)
        mixture = ref[...].astype(jnp.float32)
        mixture_ref[:, at] = mixture
        layer_ref[:, at] = (resid_ref[:, at].astype(jnp.float32) + mixture).astype(jnp.bfloat16)


def fast_body(
    hidden,
    query,
    cache_keys,
    cache_values,
    lengths,
    out_proj,
    norm_gain,
    router,
    low_factor,
    gate_weight,
    up_weight,
    down_weight,
    gate_low,
    up_low,
    experts,
):
    dev_count = lax.axis_size("dev")
    holders = dev_count // router.shape[1]
    own_rows, model_width = hidden.shape
    rows = own_rows * dev_count
    width = model_width // dev_count
    half = width // 2
    units = gate_weight.shape[1]
    rank = low_factor.shape[1]
    heads_width = query.shape[1] * query.shape[2]
    swap = [(0, 1), (1, 0)]
    bf16, f32 = jnp.bfloat16, jnp.float32
    shape = jax.ShapeDtypeStruct

    def across(value, step):
        return lax.ppermute(value, "dev", [(i, i ^ step) for i in range(dev_count)])

    def other_core(value):
        return lax.ppermute(value, "sub", swap)

    def spread(values):
        return [values[0]] + [across(values[step], step) for step in range(1, dev_count)]

    theirs = other_core(low_factor)
    sent = pl.pallas_call(
        functools.partial(attention_kernel, dev_count),
        out_shape=[shape((own_rows, heads_width + half), bf16)] * dev_count,
        in_specs=[hbm()] * 5,
        out_specs=[vmem()] * dev_count,
        scratch_shapes=[
            pltpu.SMEM(lengths.shape, jnp.int32),
            pltpu.VMEM(query.shape, bf16),
            pltpu.VMEM(cache_keys.shape, bf16),
            pltpu.VMEM(cache_values.shape, bf16),
            pltpu.VMEM(hidden.shape, bf16),
            pltpu.VMEM(query.shape, f32),
            pltpu.SemaphoreType.DMA((5,)),
        ],
        compiler_params=params(8),
        name="attention",
    )(*map(in_hbm, (lengths, query, cache_keys, cache_values, hidden)))
    got = spread(sent)

    sources = [in_hbm(gate_weight), in_hbm(up_weight), in_hbm(low_factor), theirs]

    plans = [[(0, None, (0, True)), (0, None, (0, False))]]
    seen, step, late = [0], dev_count // 2, []
    while step:
        new = [owner ^ step for owner in seen]
        early = [(0, k, (owner, True)) for k, owner in enumerate(new)]
        plans.append(late + early)
        late = [(1, k, (owner, False)) for k, owner in enumerate(new)]
        seen, step = seen + new, step // 2
    plans.append([(0,) + piece[1:] for piece in late])
    ready, pieces = [], []
    for plan in plans:
        count = READY[min(len(ready), len(READY) - 1)]
        chosen = plan[: min(count, len(plan))]
        ready.append([len(pieces) + k for k in range(len(chosen))])
        pieces += [piece[2] for piece in chosen]

    gain = norm_gain.reshape(1, model_width)
    small_inputs = [in_hbm(value) for value in (out_proj, router.T, gain, gate_low, up_low)]
    held_shapes = [
        shape((len(pieces), half, units), bf16),
        shape((len(pieces), half, units), bf16),
        shape((len(pieces), half, rank), bf16),
    ]
    fetched = pl.pallas_call(
        functools.partial(prefetch_kernel, pieces),
        out_shape=held_shapes + [shape(value.shape, value.dtype) for value in small_inputs],
        in_specs=[hbm()] * (5 + len(small_inputs)),
        out_specs=[vmem()] * (3 + len(small_inputs)),
        scratch_shapes=[
            pltpu.SemaphoreType.DMA((len(pieces), 3)),
            pltpu.SemaphoreType.DMA((len(small_inputs),)),
        ],
        compiler_params=params(2),
        cost_estimate=cost(0, 4 * len(pieces) * half * units),
        name="prefetch",
    )(sent[0], *sources, *small_inputs)
    held, (projection_weight, router_rows, gain, gate_low, up_low) = fetched[:3], fetched[3:]

    partial_proj = pl.pallas_call(
        functools.partial(projection_kernel, dev_count),
        out_shape=shape((rows, width), f32),
        in_specs=[vmem()] * (1 + dev_count),
        out_specs=vmem(),
        scratch_shapes=[pltpu.VMEM((rows, heads_width), bf16)],
        compiler_params=params(4),
        cost_estimate=cost(2 * rows * out_proj.size, 2 * out_proj.size),
        name="projection",
    )(projection_weight, *got)
    full, own_half = pl.pallas_call(
        residual_kernel,
        out_shape=[shape((rows, width), bf16), shape((rows, half), bf16)],
        in_specs=[vmem()] * 2,
        out_specs=[vmem()] * 2,
        scratch_shapes=[pltpu.VMEM((rows, width), f32)],
        compiler_params=params(4),
        name="residual",
    )(partial_proj, other_core(partial_proj))

    state_shapes = [
        shape((rows, units), f32),
        shape((rows, units), f32),
        shape((rows, rank + 2 * LANES), f32),
        shape((own_rows, model_width), bf16),
    ]

    def expert_in(number, operands, state, last_inputs=None):
        plan = plans[number]
        first, last = state is None, last_inputs is not None
        inputs = sources + list(held) + [router_rows, gain] + operands
        specs = [hbm()] * 4 + [vmem()] * (5 + len(operands))
        if not first:
            inputs += state
            specs += [vmem()] * 4
        scratch = []
        if last:
            inputs += last_inputs
            specs += [hbm()] + [vmem()] * 2
            out_shape = [shape((rows, units), bf16), shape((own_rows, LANES), f32), state_shapes[3]]
            scratch = [pltpu.VMEM(kept.shape, f32) for kept in state_shapes[:3]]
            scratch += [pltpu.SMEM(experts.shape[::-1], jnp.int32), pltpu.SemaphoreType.DMA]
        else:
            out_shape = state_shapes
        streamed = len(plan) - len(ready[number])
        if streamed:
            scratch += [
                pltpu.VMEM((streamed, half, units), bf16),
                pltpu.VMEM((streamed, half, units), bf16),
                pltpu.VMEM((streamed, half, rank), bf16),
                pltpu.SemaphoreType.DMA((streamed, 3)),
            ]
        depth = len(plan) * half
        limit = 5 + 2 * last + -(-streamed * half * (4 * units + 2 * rank) // MIB)
        return pl.pallas_call(
            functools.partial(expert_in_kernel, plan, ready[number], first, last),
            out_shape=out_shape,
            in_specs=specs,
            out_specs=[vmem()] * len(out_shape),
            scratch_shapes=scratch,
            compiler_params=params(limit),
            cost_estimate=cost(4 * rows * depth * units, 4 * depth * units),
            name="expert_in_%d" % number,
        )(*inputs)

    held_columns = own_half[None]
    step = dev_count // 2
    arrived = across(held_columns, step)
    state = expert_in(0, [full], None)
    state, arrived = lax.optimization_barrier((state, arrived))
    late, number = None, 1
    while step:
        arrived_other = other_core(arrived)
        operands = [arrived] + ([] if late is None else [late])
        held_columns = jnp.concatenate([held_columns, arrived])
        step //= 2
        coming = across(held_columns, step) if step else None
        state = expert_in(number, operands, state)
        number += 1
        state, arrived, late = lax.optimization_barrier((state, coming, arrived_other))
    inner, share, resid = expert_in(number, [late], state, [in_hbm(experts.T), gate_low, up_low])

    block = 512 if (model_width // 2) % 512 == 0 else model_width // 2
    blocks = model_width // 2 // block

    def expert_out(own):
        return pl.pallas_call(
            functools.partial(expert_out_kernel, own),
            out_shape=shape((rows, model_width // 2), f32 if own else bf16),
            in_specs=[hbm(), vmem()],
            out_specs=vmem(),
            scratch_shapes=[pltpu.VMEM((blocks, units, block), bf16), pltpu.SemaphoreType.DMA((blocks,))],
            compiler_params=params(18),
            cost_estimate=cost(rows * model_width * units, model_width * units),
            name="expert_out_own" if own else "expert_out_other",
        )(in_hbm(down_weight), inner)

    from_other = other_core(expert_out(False))
    parts = pl.pallas_call(
        functools.partial(split_kernel, dev_count),
        out_shape=[shape((own_rows, model_width // 2), bf16)] * dev_count,
        in_specs=[vmem()] * 2,
        out_specs=[vmem()] * dev_count,
        compiler_params=params(4),
        name="split",
    )(expert_out(True), from_other)
    mine = pl.pallas_call(
        functools.partial(mixture_kernel, holders),
        out_shape=shape((own_rows, model_width // 2), bf16),
        in_specs=[vmem()] * (1 + dev_count),
        out_specs=vmem(),
        compiler_params=params(4),
        name="mixture",
    )(share, *spread(parts))
    return pl.pallas_call(
        output_kernel,
        out_shape=[shape((own_rows, model_width), bf16), shape((own_rows, model_width), f32)],
        in_specs=[vmem()] * 3,
        out_specs=[vmem()] * 2,
        compiler_params=params(4),
        name="output",
    )(mine, other_core(mine), resid)


def expert_shard(row_block, low_rank, gate_weight, up_weight, down_weight, gate_low, up_low):
    gate_sum = jnp.dot(row_block, gate_weight, preferred_element_type=jnp.float32) + jnp.dot(
        low_rank, gate_low, preferred_element_type=jnp.float32
    )
    up_sum = jnp.dot(row_block, up_weight, preferred_element_type=jnp.float32) + jnp.dot(
        low_rank, up_low, preferred_element_type=jnp.float32
    )
    inner_act = (jax.nn.silu(gate_sum) * up_sum).astype(jnp.bfloat16)
    return jnp.dot(inner_act, down_weight, preferred_element_type=jnp.float32)


def route_gates(normed, router, experts):
    logits = jnp.dot(normed, router, preferred_element_type=jnp.float32)
    labels = lax.broadcasted_iota(jnp.int32, (1, 1, router.shape[1]), 2)
    picked = (experts[:, :, None] == labels).astype(jnp.float32)
    chosen = jnp.sum(logits[:, None, :] * picked, axis=-1)
    leading = jax.nn.sigmoid(chosen[:, 0] - chosen[:, 1])
    return jnp.stack([leading, 1.0 - leading], axis=-1)


def general_body(
    hidden,
    query,
    cache_keys,
    cache_values,
    lengths,
    out_proj,
    norm_gain,
    router,
    low_factor,
    gate_weight,
    up_weight,
    down_weight,
    gate_low,
    up_low,
    experts,
):
    requests = hidden.shape[0]
    model_width = hidden.shape[1]
    heads_here = query.shape[1]
    kv_here = cache_keys.shape[1]
    span_len = cache_keys.shape[2]
    head_size = query.shape[2]
    grouped = query.reshape(requests, kv_here, heads_here // kv_here, head_size)
    scores = jnp.einsum(
        "rkgd,rkld->rkgl", grouped, cache_keys, preferred_element_type=jnp.float32
    ) * head_size ** (-0.5)
    visible = lax.broadcasted_iota(jnp.int32, (requests, span_len), 1) < lengths[:, None]
    scores = jnp.where(visible[:, None, None, :], scores, -1e30)
    attn_probs = jax.nn.softmax(scores, axis=-1).astype(jnp.bfloat16)
    attended = jnp.einsum(
        "rkgl,rkld->rkgd", attn_probs, cache_values, preferred_element_type=jnp.float32
    )
    attended = attended.astype(jnp.bfloat16).reshape(requests, heads_here * head_size)
    columns = jnp.dot(
        lax.all_gather(attended, "dev", axis=0, tiled=True),
        out_proj,
        preferred_element_type=jnp.float32,
    )
    partial_proj = lax.all_to_all(columns, "dev", split_axis=0, concat_axis=1, tiled=True)
    residual = hidden.astype(jnp.float32) + lax.psum(partial_proj, "sub")
    inverse = lax.rsqrt(jnp.mean(residual * residual, axis=-1, keepdims=True) + EPSILON)
    normed = (residual * inverse * norm_gain).astype(jnp.bfloat16)
    half_width = low_factor.shape[0]
    normed_half = lax.dynamic_slice_in_dim(
        normed, lax.axis_index("sub") * half_width, half_width, 1
    )
    low_partial = jnp.dot(normed_half, low_factor, preferred_element_type=jnp.float32)
    low_rank = lax.psum(low_partial, "sub").astype(jnp.bfloat16)
    rank_width = low_rank.shape[1]
    expert_count = router.shape[1]
    holders = lax.axis_size("dev") // expert_count
    gate_pair = route_gates(normed, router, experts)
    flat_ids = experts.reshape(-1)
    entries = flat_ids.shape[0]
    same_expert = flat_ids[:, None] == flat_ids[None, :]
    earlier = lax.broadcasted_iota(jnp.int32, (entries, entries), 0) > lax.broadcasted_iota(
        jnp.int32, (entries, entries), 1
    )
    slot_index = jnp.sum((same_expert & earlier).astype(jnp.int32), axis=1).reshape(requests, 2)
    target = experts * CAP + slot_index
    placement = (
        target[:, :, None] == lax.broadcasted_iota(jnp.int32, (1, 1, expert_count * CAP), 2)
    ).astype(jnp.float32)
    chosen = jnp.sum(placement, axis=1).astype(jnp.bfloat16)
    packed_rows = jnp.einsum(
        "rs,rd->sd", chosen, normed, preferred_element_type=jnp.float32
    ).astype(jnp.bfloat16)
    packed_low = jnp.einsum(
        "rs,rd->sd", chosen, low_rank, preferred_element_type=jnp.float32
    ).astype(jnp.bfloat16)
    send_rows = jnp.repeat(packed_rows.reshape(expert_count, CAP, model_width), holders, axis=0)
    send_low = jnp.repeat(packed_low.reshape(expert_count, CAP, rank_width), holders, axis=0)
    got_rows = lax.all_to_all(send_rows, "dev", split_axis=0, concat_axis=0, tiled=True)
    got_low = lax.all_to_all(send_low, "dev", split_axis=0, concat_axis=0, tiled=True)
    sources = got_rows.shape[0]
    slot_count = got_rows.shape[1]
    result = expert_shard(
        got_rows.reshape(sources * slot_count, model_width),
        got_low.reshape(sources * slot_count, rank_width),
        gate_weight,
        up_weight,
        down_weight,
        gate_low,
        up_low,
    )
    partials = result.reshape(sources, slot_count, model_width)
    returned = lax.all_to_all(
        partials.astype(jnp.bfloat16), "dev", split_axis=0, concat_axis=0, tiled=True
    ).astype(partials.dtype)
    per_slot = jnp.sum(returned.reshape(expert_count, holders, CAP, model_width), axis=1).reshape(
        expert_count * CAP, model_width
    )
    weighted = jnp.sum(placement * gate_pair[:, :, None], axis=1)
    mixture_part = jnp.dot(weighted, per_slot, precision=lax.Precision.HIGHEST)
    mixture = lax.psum(mixture_part.astype(jnp.bfloat16), "sub").astype(jnp.float32)
    return ((residual + mixture).astype(jnp.bfloat16), mixture)


def body(*arrays):
    hidden, query, out_proj, router, units = arrays[0], arrays[1], arrays[5], arrays[7], arrays[9].shape[1]
    dev_count = lax.axis_size("dev")
    fits = (
        lax.axis_size("sub") == 2
        and dev_count >= 4
        and dev_count & (dev_count - 1) == 0
        and dev_count % router.shape[1] == 0
        and hidden.shape[0] == 8
        and hidden.shape[1] % (4 * LANES * dev_count) in (0, 2 * LANES * dev_count)
        and hidden.shape[1] * units <= 6144 * 2048
        and query.shape[2] == LANES
    )
    return (fast_body if fits else general_body)(*arrays)


def solution(mesh):
    placed = (
        P(("groups", "dev"), None),
        P(("groups", "dev"), "sub", None),
        P(("groups", "dev"), "sub", None, None),
        P(("groups", "dev"), "sub", None, None),
        P(("groups", "dev")),
        P("sub", "dev"),
        P(),
        P(),
        P("sub", None),
        P(None, ("dev", "sub")),
        P(None, ("dev", "sub")),
        P(("dev", "sub"), None),
        P(None, ("dev", "sub")),
        P(None, ("dev", "sub")),
        P(("groups", "dev"), None),
    )
    return jax.shard_map(
        body,
        mesh=mesh,
        in_specs=placed,
        out_specs=(P(("groups", "dev"), None), P(("groups", "dev"), None)),
        check_vma=False,
    )
```

```python
import functools

import jax
import jax.numpy as jnp
from jax import lax
from jax.experimental import pallas as pl
from jax.experimental.pallas import tpu as pltpu
from jax.sharding import PartitionSpec as P

CAP = 6
EPSILON = 1e-05
READY = (1, 0, 1, 2, 2)
PREFETCH_FIRST = 2
MIB = 1 << 20
LANES = 128


def vmem():
    return pl.BlockSpec(memory_space=pltpu.VMEM)


def hbm():
    return pl.BlockSpec(memory_space=pltpu.HBM)


def in_hbm(value):
    return pltpu.with_memory_space_constraint(value, pltpu.HBM)


def params(limit_mib):
    return pltpu.CompilerParams(vmem_limit_bytes=limit_mib * MIB)


def cost(flops, bytes_accessed):
    return pl.CostEstimate(flops=int(flops), bytes_accessed=int(bytes_accessed), transcendentals=0)


def attention_kernel(
    dev_count, steps, lengths_hbm, query_hbm, keys_hbm, values_hbm, hidden_hbm, *refs
):
    out_refs, refs = refs[: len(steps)], refs[len(steps) :]
    lengths_ref, query_ref, keys_ref, values_ref, hidden_ref, rows_ref, sems = refs
    me, sub = lax.axis_index("dev"), lax.axis_index("sub")
    requests, heads, head_size = query_ref.shape
    kv_heads, span = keys_ref.shape[1], keys_ref.shape[2]
    group = heads // kv_heads
    slots = kv_heads * span
    copies = [
        pltpu.make_async_copy(source, target, sems.at[number])
        for number, (source, target) in enumerate(
            (
                (lengths_hbm, lengths_ref),
                (query_hbm, query_ref),
                (keys_hbm, keys_ref),
                (values_hbm, values_ref),
                (hidden_hbm, hidden_ref),
            )
        )
    ]
    for copy in copies:
        copy.start()
    column = lax.broadcasted_iota(jnp.int32, (heads, slots), 1)
    owner = lax.broadcasted_iota(jnp.int32, (heads, slots), 0) // group
    position = column - owner * span
    for copy in copies[:3]:
        copy.wait()
    scores = [
        lax.dot_general(
            query_ref[r],
            keys_ref[r].reshape(slots, head_size),
            (((1,), (1,)), ((), ())),
            preferred_element_type=jnp.float32,
        )
        for r in range(requests)
    ]
    probs = []
    for r in range(requests):
        visible = (position >= 0) & (position < jnp.minimum(lengths_ref[r], span))
        score = jnp.where(visible, scores[r] * head_size ** (-0.5), -1e30)
        weight = jnp.exp(score - jnp.max(score, axis=1, keepdims=True))
        probs.append((weight / jnp.sum(weight, axis=1, keepdims=True)).astype(jnp.bfloat16))
    copies[3].wait()
    for r in range(requests):
        rows_ref[r] = jnp.dot(
            probs[r], values_ref[r].reshape(slots, head_size), preferred_element_type=jnp.float32
        )
    for h in range(heads):
        value = rows_ref[:, h, :].astype(jnp.bfloat16)
        for out_ref in out_refs:
            out_ref[:, h * head_size : (h + 1) * head_size] = value
    half = hidden_ref.shape[1] // (2 * dev_count)
    copies[4].wait()
    for out_ref, peers in zip(out_refs, steps):
        for number, peer in enumerate(peers):
            at = pl.multiple_of(((me ^ peer) * 2 + sub) * half, LANES)
            to = heads * head_size + number * half
            out_ref[:, to : to + half] = hidden_ref[:, pl.ds(at, half)]


def half_block(piece, width):
    sub = lax.axis_index("sub")
    side = sub if piece[1] else 1 - sub
    return pl.multiple_of(((lax.axis_index("dev") ^ piece[0]) * 2 + side) * width, LANES)


def weight_copies(piece, sources, targets, sems):
    width = targets[0].shape[0]
    at = pl.ds(half_block(piece, width), width)
    return [
        pltpu.make_async_copy(source.at[at, :], target, sems.at[number])
        for number, (source, target) in enumerate(zip(sources, targets))
    ]


def prefetch_kernel(pieces, plain, after_ref, *refs):
    sources, outputs, sems, plain_sems = refs[: 2 + plain], refs[2 + plain : -2], refs[-2], refs[-1]
    copies = [
        pltpu.make_async_copy(source, target, plain_sems.at[number])
        for number, (source, target) in enumerate(zip(sources[2:], outputs[2:]))
    ]
    for index, piece in enumerate(pieces):
        copies += weight_copies(piece, sources[:2], [ref.at[index] for ref in outputs[:2]], sems.at[index])
    for copy in copies:
        copy.start()
    for copy in copies:
        copy.wait()


def join_kernel(width, *refs):
    out_ref, at = refs[-1], 0
    for ref in refs[:-1]:
        out_ref[at : at + ref.shape[0]] = ref[...] if width is None else ref[:, :width]
        at += ref.shape[0]


def projection_kernel(origins, weight_ref, *refs):
    got_refs, (out_ref, stacked) = refs[:-2], refs[-2:]
    me, sub = lax.axis_index("dev"), lax.axis_index("sub")
    own_rows = out_ref.shape[0] // len(origins)
    depth = weight_ref.shape[0]
    half = out_ref.shape[1] // 2
    for number, (operand, row, _, _) in enumerate(origins):
        stacked[number * own_rows : (number + 1) * own_rows, :] = got_refs[operand][row : row + own_rows, :depth]
    product = jnp.dot(stacked[...], weight_ref[...], preferred_element_type=jnp.float32)
    columns = pl.ds(pl.multiple_of(sub * half, LANES), half)
    for number, (operand, row, column, owner) in enumerate(origins):
        rows = pl.ds(pl.multiple_of((me ^ owner) * own_rows, own_rows), own_rows)
        piece = got_refs[operand][row : row + own_rows, column : column + half].astype(jnp.float32)
        out_ref[rows, :] = product[number * own_rows : (number + 1) * own_rows, :]
        out_ref[rows, columns] = out_ref[rows, columns] + piece


def residual_kernel(mine_ref, other_ref, full_ref, half_ref, sums):
    sub = lax.axis_index("sub")
    half = half_ref.shape[1]
    sums[...] = mine_ref[...] + other_ref[...]
    full_ref[...] = sums[...].astype(jnp.bfloat16)
    half_ref[...] = sums[:, pl.ds(pl.multiple_of(sub * half, LANES), half)].astype(jnp.bfloat16)


def expert_in_kernel(plan, places, groups, width, first, last, *refs):
    refs = list(refs)

    def take(count):
        taken, refs[:] = refs[:count], refs[count:]
        return taken

    operands = 1 + max(piece[0] for piece in plan)
    sources = take(2)
    held = [take(2) for _ in range(groups)]
    mine_ref, theirs_ref, router_ref, gain_ref = take(4)
    x_refs = take(operands)
    before = None if first else take(4)
    if last:
        last_sources = take(3)
        inner_ref, share_ref, resid_ref = take(3)
    else:
        gate_sum, up_sum, small, resid_ref = take(4)
    streamed = [piece[2] for piece, place in zip(plan, places) if place is None]
    copies = []
    if streamed:
        gate_buf, up_buf, sems = take(3)
        copies = [
            weight_copies(piece, sources, [gate_buf.at[slot], up_buf.at[slot]], sems.at[slot])
            for slot, piece in enumerate(streamed)
        ]
        for copy in sum(copies[:2], []):
            copy.start()
    if last:
        gate_sum, up_sum, small, names, gate_low_ref, up_low_ref, last_sems = take(7)
        last_copies = [
            pltpu.make_async_copy(source, target, last_sems.at[number])
            for number, (source, target) in enumerate(zip(last_sources, (names, gate_low_ref, up_low_ref)))
        ]
        for copy in last_copies:
            copy.start()
    me, sub = lax.axis_index("dev"), lax.axis_index("sub")
    rank, experts = mine_ref.shape[1], router_ref.shape[0]
    factor_rows = mine_ref.shape[0]
    own_rows, model_width = resid_ref.shape
    if first:
        gate_sum[...] = jnp.zeros_like(gate_sum)
        up_sum[...] = jnp.zeros_like(up_sum)
        small[...] = jnp.zeros_like(small)
    else:
        for now, earlier in zip((gate_sum, up_sum, small, resid_ref), before):
            now[...] = earlier[...]
    my_rows = pl.ds(pl.multiple_of(me * own_rows, own_rows), own_rows)
    slot = 0
    for (operand, which, piece), place in zip(plan, places):
        base = half_block(piece, width)
        if which is None:
            side = sub if piece[1] else 1 - sub
            source, columns = x_refs[operand], pl.ds(pl.multiple_of(side * width, LANES), width)
        else:
            source, columns = x_refs[operand].at[which], slice(0, width)
        x = source[:, columns].astype(jnp.float32)
        small[:, rank + LANES :] += jnp.sum(x * x, axis=1, keepdims=True)
        resid_ref[:, pl.ds(base, width)] = source[my_rows, columns]
        x = (x * gain_ref[:, pl.ds(base, width)]).astype(jnp.bfloat16)
        small[:, rank : rank + experts] += lax.dot_general(
            x, router_ref[:, pl.ds(base, width)], (((1,), (1,)), ((), ())), preferred_element_type=jnp.float32
        )
        if place is None:
            gate_ref, up_ref, index = gate_buf, up_buf, slot
            for copy in copies[slot]:
                copy.wait()
            slot += 1
            for copy in sum(copies[slot + 1 : slot + 2], []):
                copy.start()
        else:
            (gate_ref, up_ref), index = held[place[0]], place[1]
        upper = base >= factor_rows
        at = pl.ds(pl.multiple_of(jnp.where(upper, base - factor_rows, base), LANES), width)
        factor = jnp.where(upper == (sub == 1), mine_ref[at, :], theirs_ref[at, :])
        small[:, :rank] += jnp.dot(x, factor, preferred_element_type=jnp.float32)
        gate_sum[...] += jnp.dot(x, gate_ref[index], preferred_element_type=jnp.float32)
        up_sum[...] += jnp.dot(x, up_ref[index], preferred_element_type=jnp.float32)
    if not last:
        return
    for copy in last_copies:
        copy.wait()
    inverse = lax.rsqrt(small[:, rank + LANES : rank + LANES + 1] / model_width + EPSILON)
    low_rank = (small[:, :rank] * inverse).astype(jnp.bfloat16)
    gate = gate_sum[...] * inverse + jnp.dot(
        low_rank, gate_low_ref[...], preferred_element_type=jnp.float32
    )
    up = up_sum[...] * inverse + jnp.dot(
        low_rank, up_low_ref[...], preferred_element_type=jnp.float32
    )
    inner_ref[...] = (jax.nn.silu(gate) * up).astype(jnp.bfloat16)
    mine = small[my_rows, :]
    inverse = lax.rsqrt(mine[:, rank + LANES : rank + LANES + 1] / model_width + EPSILON)
    logits = mine[:, rank : rank + LANES] * inverse
    lanes = lax.broadcasted_iota(jnp.int32, (own_rows, LANES), 1)
    numbers = lax.broadcasted_iota(jnp.int32, (own_rows, LANES), 0)
    one, two = jnp.zeros_like(numbers), jnp.zeros_like(numbers)
    for r in range(own_rows):
        one = jnp.where(numbers == r, names[0, r], one)
        two = jnp.where(numbers == r, names[1, r], two)
    chosen_one = jnp.sum(jnp.where(lanes == one, logits, 0.0), axis=1, keepdims=True)
    chosen_two = jnp.sum(jnp.where(lanes == two, logits, 0.0), axis=1, keepdims=True)
    leading = jax.nn.sigmoid(chosen_one - chosen_two)
    share_ref[...] = jnp.where(lanes == one, leading, 0.0) + jnp.where(lanes == two, 1.0 - leading, 0.0)


def expert_out_kernel(own, down_ref, inner_ref, out_ref, sums, buf, sems):
    blocks, block, columns = buf.shape
    sub = lax.axis_index("sub")
    start = pl.multiple_of((sub if own else 1 - sub) * columns, LANES)
    copies = [
        pltpu.make_async_copy(
            down_ref.at[index * block : (index + 1) * block, pl.ds(start, columns)], buf.at[index], sems.at[index]
        )
        for index in range(blocks)
    ]
    for copy in copies[:3]:
        copy.start()
    for index in range(blocks):
        copies[index].wait()
        for copy in copies[index + 3 : index + 4]:
            copy.start()
        inner = inner_ref[:, index * block : (index + 1) * block]
        product = jnp.dot(inner, buf[index], preferred_element_type=jnp.float32)
        sums[...] = product if index == 0 else sums[...] + product
    out_ref[...] = sums[...].astype(out_ref.dtype)


def split_kernel(mine_ref, other_ref, out_ref):
    peers, rows, _ = out_ref.shape
    for peer in range(peers):
        at = slice(peer * rows, (peer + 1) * rows)
        out_ref[peer] = (mine_ref[at, :] + other_ref[at, :].astype(jnp.float32)).astype(jnp.bfloat16)


def mixture_kernel(holders, share_ref, parts_ref, out_ref):
    total = jnp.zeros(out_ref.shape, jnp.float32)
    for expert in range(parts_ref.shape[0] // holders):
        held = parts_ref[expert * holders].astype(jnp.float32)
        for holder in range(1, holders):
            held = held + parts_ref[expert * holders + holder].astype(jnp.float32)
        total = total + held * share_ref[:, expert : expert + 1]
    out_ref[...] = total.astype(jnp.bfloat16)


def output_kernel(mine_ref, other_ref, resid_ref, layer_ref, mixture_ref):
    sub = lax.axis_index("sub")
    half = mine_ref.shape[1]
    for ref, side in ((mine_ref, sub), (other_ref, 1 - sub)):
        at = pl.ds(pl.multiple_of(side * half, LANES), half)
        mixture = ref[...].astype(jnp.float32)
        mixture_ref[:, at] = mixture
        layer_ref[:, at] = (resid_ref[:, at].astype(jnp.float32) + mixture).astype(jnp.bfloat16)


def fast_body(
    hidden,
    query,
    cache_keys,
    cache_values,
    lengths,
    out_proj,
    norm_gain,
    router,
    low_factor,
    gate_weight,
    up_weight,
    down_weight,
    gate_low,
    up_low,
    experts,
):
    dev_count = lax.axis_size("dev")
    holders = dev_count // router.shape[1]
    own_rows, model_width = hidden.shape
    rows = own_rows * dev_count
    width = model_width // dev_count
    half = width // 2
    units = gate_weight.shape[1]
    rank = low_factor.shape[1]
    heads_width = query.shape[1] * query.shape[2]
    bf16, f32 = jnp.bfloat16, jnp.float32
    shape = jax.ShapeDtypeStruct

    def across(value, step):
        return lax.ppermute(value, "dev", [(i, i ^ step) for i in range(dev_count)])

    def other_core(value):
        return lax.ppermute(value, "sub", [(0, 1), (1, 0)])

    def join(values, columns=None):
        kind = values[0].shape[1:] if columns is None else (columns,)
        return pl.pallas_call(
            functools.partial(join_kernel, columns),
            out_shape=shape((sum(value.shape[0] for value in values),) + kind, bf16),
            in_specs=[vmem()] * len(values),
            out_specs=vmem(),
            compiler_params=params(2),
            name="join",
        )(*values)

    bits = []
    while 2 << len(bits) < dev_count:
        bits.insert(0, 2 << len(bits))
    seen, paired, plans = [0], [], [[(0, None, (0, True)), (0, None, (0, False))]]
    stages = []
    fresh, late = [0], []
    for bit in bits + [None]:
        arrived = [] if bit is None else [owner ^ bit for owner in seen]
        turned = [owner ^ 1 for owner in fresh]
        stages.append((bit, arrived, turned))
        early = [(0, k, (owner, True)) for k, owner in enumerate(arrived + turned)]
        plans.append(late + early)
        late = [(1, k, (owner, False)) for k, owner in enumerate(arrived + turned)]
        seen, fresh = seen + arrived, arrived
    plans.append([(0,) + piece[1:] for piece in late])

    ready = [piece[2] for plan, count in zip(plans, READY) for piece in plan[:count]]
    pieces_of = [ready[:PREFETCH_FIRST], ready[PREFETCH_FIRST:]]
    where = {piece: (group, index) for group in range(2) for index, piece in enumerate(pieces_of[group])}

    theirs = other_core(low_factor)
    sources = [in_hbm(gate_weight), in_hbm(up_weight)]

    upper = list(range(2, dev_count, 2))
    steps = [(0,), (1,)] + [(step ^ 1, step) for step in upper]
    sent = pl.pallas_call(
        functools.partial(attention_kernel, dev_count, steps),
        out_shape=[shape((own_rows, heads_width + half * len(peers)), bf16) for peers in steps],
        in_specs=[hbm()] * 5,
        out_specs=[vmem()] * len(steps),
        scratch_shapes=[
            pltpu.SMEM(lengths.shape, jnp.int32),
            pltpu.VMEM(query.shape, bf16),
            pltpu.VMEM(cache_keys.shape, bf16),
            pltpu.VMEM(cache_values.shape, bf16),
            pltpu.VMEM(hidden.shape, bf16),
            pltpu.VMEM(query.shape, f32),
            pltpu.SemaphoreType.DMA((5,)),
        ],
        compiler_params=params(8),
        name="attention",
    )(*map(in_hbm, (lengths, query, cache_keys, cache_values, hidden)))

    def prefetch(group, after, plain):
        pieces = pieces_of[group]
        return pl.pallas_call(
            functools.partial(prefetch_kernel, pieces, len(plain)),
            out_shape=[shape((len(pieces), half, units), bf16)] * 2
            + [shape(value.shape, value.dtype) for value in plain],
            in_specs=[vmem()] + [hbm()] * (2 + len(plain)),
            out_specs=[vmem()] * (2 + len(plain)),
            scratch_shapes=[pltpu.SemaphoreType.DMA((len(pieces), 2)), pltpu.SemaphoreType.DMA((max(1, len(plain)),))],
            compiler_params=params(2),
            cost_estimate=cost(0, 4 * len(pieces) * half * units),
            name="prefetch_%d" % group,
        )(after, *sources, *plain)

    got = [across(sent[2 + k], step) for k, step in enumerate(upper)]
    got_pair = across(sent[1], 1)
    gain = norm_gain.reshape(1, model_width)
    fetched = prefetch(0, sent[0], [in_hbm(value) for value in (out_proj, low_factor, router.T, gain)])
    held, (projection_weight, factor, router_rows, gain) = [fetched[:2]], fetched[2:]
    got, got_pair, gain = lax.optimization_barrier((got, got_pair, gain))
    packed = join(got, heads_width + half)
    got_packed = across(packed, 1)
    held.append(prefetch(1, packed, []))
    projection_weight, held[1] = lax.optimization_barrier((projection_weight, held[1]))

    origins = [(0, 0, heads_width, 0), (1, 0, heads_width, 1)]
    origins += [(2 + k, 0, heads_width + half, step) for k, step in enumerate(upper)]
    origins += [(2 + len(upper), k * own_rows, heads_width, step ^ 1) for k, step in enumerate(upper)]
    partial_proj = pl.pallas_call(
        functools.partial(projection_kernel, origins),
        out_shape=shape((rows, width), f32),
        in_specs=[vmem()] * (4 + len(upper)),
        out_specs=vmem(),
        scratch_shapes=[pltpu.VMEM((rows, heads_width), bf16)],
        compiler_params=params(4),
        cost_estimate=cost(2 * rows * out_proj.size, 2 * out_proj.size),
        name="projection",
    )(projection_weight, sent[0], got_pair, *got, got_packed)
    full, own_half = pl.pallas_call(
        residual_kernel,
        out_shape=[shape((rows, width), bf16), shape((rows, half), bf16)],
        in_specs=[vmem()] * 2,
        out_specs=[vmem()] * 2,
        scratch_shapes=[pltpu.VMEM((rows, width), f32)],
        compiler_params=params(4),
        name="residual",
    )(partial_proj, other_core(partial_proj))

    state_shapes = [
        shape((rows, units), f32),
        shape((rows, units), f32),
        shape((rows, rank + 2 * LANES), f32),
        shape((own_rows, model_width), bf16),
    ]

    def expert_in(number, operands, state, last_inputs=None):
        plan = plans[number]
        first, last = state is None, last_inputs is not None
        used = sorted({where[piece[2]][0] for piece in plan if piece[2] in where})
        places = [
            (used.index(where[piece[2]][0]), where[piece[2]][1]) if piece[2] in where else None for piece in plan
        ]
        streamed = places.count(None)
        inputs = list(sources)
        specs = [hbm()] * 2
        for number_used in used:
            inputs += held[number_used]
        inputs += [factor, theirs, router_rows, gain] + operands
        if not first:
            inputs += state
        specs += [vmem()] * (len(inputs) - len(specs))
        scratch = []
        if streamed:
            scratch += [pltpu.VMEM((streamed, half, units), bf16)] * 2 + [pltpu.SemaphoreType.DMA((streamed, 2))]
        if last:
            inputs += last_inputs
            specs += [hbm()] * 3
            out_shape = [shape((rows, units), bf16), shape((own_rows, LANES), f32), state_shapes[3]]
            scratch += [pltpu.VMEM(kept.shape, f32) for kept in state_shapes[:3]]
            scratch += [pltpu.SMEM(experts.shape[::-1], jnp.int32)]
            scratch += [pltpu.VMEM((rank, units), bf16)] * 2 + [pltpu.SemaphoreType.DMA((3,))]
        else:
            out_shape = list(state_shapes)
        depth = len(plan) * half
        limit = 4 + 5 * last + -(-streamed * half * units * 4 // MIB)
        result = pl.pallas_call(
            functools.partial(expert_in_kernel, plan, places, len(used), half, first, last),
            out_shape=out_shape,
            in_specs=specs,
            out_specs=[vmem()] * len(out_shape),
            scratch_shapes=scratch,
            compiler_params=params(limit),
            cost_estimate=cost(4 * rows * depth * units, 4 * depth * units),
            name="expert_in_%d" % number,
        )(*inputs)
        return list(result)

    have, fresh, late, state = own_half[None], own_half[None], None, None
    for number, (bit, arrived, turned) in enumerate(stages):
        flying = [] if bit is None else [across(have, bit)]
        flying.append(across(fresh, 1))
        late_now = late
        operands = [full] if number == 0 else [new] + ([] if late_now is None else [late_now])
        state = expert_in(number, operands, state)
        if number:
            late_sent = other
        else:
            late_sent = None
        state, flying, late = lax.optimization_barrier((state, flying, late_sent))
        new = join(flying) if len(flying) > 1 else flying[0]
        other = other_core(new)
        if bit is not None:
            fresh = flying[0]
            have = join([have, fresh])
    number = len(stages)
    state = expert_in(number, [new] + ([] if late is None else [late]), state)
    state, other = lax.optimization_barrier((state, other))
    inner, share, resid = expert_in(number + 1, [other], state, [in_hbm(value) for value in (experts.T, gate_low, up_low)])

    def expert_out(own):
        return pl.pallas_call(
            functools.partial(expert_out_kernel, own),
            out_shape=shape((rows, model_width // 2), f32 if own else bf16),
            in_specs=[hbm(), vmem()],
            out_specs=vmem(),
            scratch_shapes=[
                pltpu.VMEM((rows, model_width // 2), f32),
                pltpu.VMEM((8, units // 8, model_width // 2), bf16),
                pltpu.SemaphoreType.DMA((8,)),
            ],
            compiler_params=params(18),
            cost_estimate=cost(rows * model_width * units, model_width * units),
            name="expert_out_own" if own else "expert_out_other",
        )(in_hbm(down_weight), inner)

    from_other = other_core(expert_out(False))
    own_sum = expert_out(True)
    parts = pl.pallas_call(
        split_kernel,
        out_shape=shape((dev_count, own_rows, model_width // 2), bf16),
        in_specs=[vmem()] * 2,
        out_specs=vmem(),
        compiler_params=params(4),
        name="split",
    )(own_sum, from_other)
    parts = lax.all_to_all(parts, "dev", split_axis=0, concat_axis=0, tiled=True)
    mine = pl.pallas_call(
        functools.partial(mixture_kernel, holders),
        out_shape=shape((own_rows, model_width // 2), bf16),
        in_specs=[vmem()] * 2,
        out_specs=vmem(),
        compiler_params=params(4),
        name="mixture",
    )(share, parts)
    return pl.pallas_call(
        output_kernel,
        out_shape=[shape((own_rows, model_width), bf16), shape((own_rows, model_width), f32)],
        in_specs=[vmem()] * 3,
        out_specs=[vmem()] * 2,
        compiler_params=params(4),
        name="output",
    )(mine, other_core(mine), resid)


def expert_shard(row_block, low_rank, gate_weight, up_weight, down_weight, gate_low, up_low):
    gate_sum = jnp.dot(row_block, gate_weight, preferred_element_type=jnp.float32) + jnp.dot(
        low_rank, gate_low, preferred_element_type=jnp.float32
    )
    up_sum = jnp.dot(row_block, up_weight, preferred_element_type=jnp.float32) + jnp.dot(
        low_rank, up_low, preferred_element_type=jnp.float32
    )
    inner_act = (jax.nn.silu(gate_sum) * up_sum).astype(jnp.bfloat16)
    return jnp.dot(inner_act, down_weight, preferred_element_type=jnp.float32)


def route_gates(normed, router, experts):
    logits = jnp.dot(normed, router, preferred_element_type=jnp.float32)
    labels = lax.broadcasted_iota(jnp.int32, (1, 1, router.shape[1]), 2)
    picked = (experts[:, :, None] == labels).astype(jnp.float32)
    chosen = jnp.sum(logits[:, None, :] * picked, axis=-1)
    leading = jax.nn.sigmoid(chosen[:, 0] - chosen[:, 1])
    return jnp.stack([leading, 1.0 - leading], axis=-1)


def general_body(
    hidden,
    query,
    cache_keys,
    cache_values,
    lengths,
    out_proj,
    norm_gain,
    router,
    low_factor,
    gate_weight,
    up_weight,
    down_weight,
    gate_low,
    up_low,
    experts,
):
    requests = hidden.shape[0]
    model_width = hidden.shape[1]
    heads_here = query.shape[1]
    kv_here = cache_keys.shape[1]
    span_len = cache_keys.shape[2]
    head_size = query.shape[2]
    grouped = query.reshape(requests, kv_here, heads_here // kv_here, head_size)
    scores = jnp.einsum(
        "rkgd,rkld->rkgl", grouped, cache_keys, preferred_element_type=jnp.float32
    ) * head_size ** (-0.5)
    visible = lax.broadcasted_iota(jnp.int32, (requests, span_len), 1) < lengths[:, None]
    scores = jnp.where(visible[:, None, None, :], scores, -1e30)
    attn_probs = jax.nn.softmax(scores, axis=-1).astype(jnp.bfloat16)
    attended = jnp.einsum(
        "rkgl,rkld->rkgd", attn_probs, cache_values, preferred_element_type=jnp.float32
    )
    attended = attended.astype(jnp.bfloat16).reshape(requests, heads_here * head_size)
    columns = jnp.dot(
        lax.all_gather(attended, "dev", axis=0, tiled=True),
        out_proj,
        preferred_element_type=jnp.float32,
    )
    partial_proj = lax.all_to_all(columns, "dev", split_axis=0, concat_axis=1, tiled=True)
    residual = hidden.astype(jnp.float32) + lax.psum(partial_proj, "sub")
    inverse = lax.rsqrt(jnp.mean(residual * residual, axis=-1, keepdims=True) + EPSILON)
    normed = (residual * inverse * norm_gain).astype(jnp.bfloat16)
    half_width = low_factor.shape[0]
    normed_half = lax.dynamic_slice_in_dim(
        normed, lax.axis_index("sub") * half_width, half_width, 1
    )
    low_partial = jnp.dot(normed_half, low_factor, preferred_element_type=jnp.float32)
    low_rank = lax.psum(low_partial, "sub").astype(jnp.bfloat16)
    rank_width = low_rank.shape[1]
    expert_count = router.shape[1]
    holders = lax.axis_size("dev") // expert_count
    gate_pair = route_gates(normed, router, experts)
    flat_ids = experts.reshape(-1)
    entries = flat_ids.shape[0]
    same_expert = flat_ids[:, None] == flat_ids[None, :]
    earlier = lax.broadcasted_iota(jnp.int32, (entries, entries), 0) > lax.broadcasted_iota(
        jnp.int32, (entries, entries), 1
    )
    slot_index = jnp.sum((same_expert & earlier).astype(jnp.int32), axis=1).reshape(requests, 2)
    target = experts * CAP + slot_index
    placement = (
        target[:, :, None] == lax.broadcasted_iota(jnp.int32, (1, 1, expert_count * CAP), 2)
    ).astype(jnp.float32)
    chosen = jnp.sum(placement, axis=1).astype(jnp.bfloat16)
    packed_rows = jnp.einsum(
        "rs,rd->sd", chosen, normed, preferred_element_type=jnp.float32
    ).astype(jnp.bfloat16)
    packed_low = jnp.einsum(
        "rs,rd->sd", chosen, low_rank, preferred_element_type=jnp.float32
    ).astype(jnp.bfloat16)
    send_rows = jnp.repeat(packed_rows.reshape(expert_count, CAP, model_width), holders, axis=0)
    send_low = jnp.repeat(packed_low.reshape(expert_count, CAP, rank_width), holders, axis=0)
    got_rows = lax.all_to_all(send_rows, "dev", split_axis=0, concat_axis=0, tiled=True)
    got_low = lax.all_to_all(send_low, "dev", split_axis=0, concat_axis=0, tiled=True)
    sources = got_rows.shape[0]
    slot_count = got_rows.shape[1]
    result = expert_shard(
        got_rows.reshape(sources * slot_count, model_width),
        got_low.reshape(sources * slot_count, rank_width),
        gate_weight,
        up_weight,
        down_weight,
        gate_low,
        up_low,
    )
    partials = result.reshape(sources, slot_count, model_width)
    returned = lax.all_to_all(
        partials.astype(jnp.bfloat16), "dev", split_axis=0, concat_axis=0, tiled=True
    ).astype(partials.dtype)
    per_slot = jnp.sum(returned.reshape(expert_count, holders, CAP, model_width), axis=1).reshape(
        expert_count * CAP, model_width
    )
    weighted = jnp.sum(placement * gate_pair[:, :, None], axis=1)
    mixture_part = jnp.dot(weighted, per_slot, precision=lax.Precision.HIGHEST)
    mixture = lax.psum(mixture_part.astype(jnp.bfloat16), "sub").astype(jnp.float32)
    return ((residual + mixture).astype(jnp.bfloat16), mixture)


def body(*arrays):
    hidden, query, out_proj, router, units = arrays[0], arrays[1], arrays[5], arrays[7], arrays[9].shape[1]
    dev_count = lax.axis_size("dev")
    fits = (
        lax.axis_size("sub") == 2
        and dev_count >= 4
        and dev_count & (dev_count - 1) == 0
        and dev_count % router.shape[1] == 0
        and hidden.shape[0] == 8
        and hidden.shape[1] % (4 * LANES * dev_count) in (0, 2 * LANES * dev_count)
        and hidden.shape[1] * units <= 6144 * 2048
        and query.shape[2] == LANES
    )
    return (fast_body if fits else general_body)(*arrays)


def solution(mesh):
    placed = (
        P(("groups", "dev"), None),
        P(("groups", "dev"), "sub", None),
        P(("groups", "dev"), "sub", None, None),
        P(("groups", "dev"), "sub", None, None),
        P(("groups", "dev")),
        P("sub", "dev"),
        P(),
        P(),
        P("sub", None),
        P(None, ("dev", "sub")),
        P(None, ("dev", "sub")),
        P(("dev", "sub"), None),
        P(None, ("dev", "sub")),
        P(None, ("dev", "sub")),
        P(("groups", "dev"), None),
    )
    return jax.shard_map(
        body,
        mesh=mesh,
        in_specs=placed,
        out_specs=(P(("groups", "dev"), None), P(("groups", "dev"), None)),
        check_vma=False,
    )
```

```python
import functools

import jax
import jax.numpy as jnp
from jax import lax
from jax.experimental import pallas as pl
from jax.experimental.pallas import tpu as pltpu
from jax.sharding import PartitionSpec as P

CAP = 6
EPSILON = 1e-05
READY = (1,0,1,1,2)
PREFETCH_FIRST = 1
COLUMN_PARTS = 1
DOWN_READY = 4
MIB = 1 << 20
LANES = 128


def vmem():
    return pl.BlockSpec(memory_space=pltpu.VMEM)


def hbm():
    return pl.BlockSpec(memory_space=pltpu.HBM)


def in_hbm(value):
    return pltpu.with_memory_space_constraint(value, pltpu.HBM)


def params(limit_mib):
    return pltpu.CompilerParams(vmem_limit_bytes=limit_mib * MIB)


def cost(flops, bytes_accessed):
    return pl.CostEstimate(flops=int(flops), bytes_accessed=int(bytes_accessed), transcendentals=0)


def attention_kernel(
    dev_count, steps, lengths_hbm, query_hbm, keys_hbm, values_hbm, hidden_hbm, *refs
):
    out_refs, refs = refs[: len(steps)], refs[len(steps) :]
    lengths_ref, query_ref, keys_ref, values_ref, hidden_ref, rows_ref, sems = refs
    me, sub = lax.axis_index("dev"), lax.axis_index("sub")
    requests, heads, head_size = query_ref.shape
    kv_heads, span = keys_ref.shape[1], keys_ref.shape[2]
    group = heads // kv_heads
    slots = kv_heads * span
    copies = [
        pltpu.make_async_copy(source, target, sems.at[number])
        for number, (source, target) in enumerate(
            (
                (lengths_hbm, lengths_ref),
                (query_hbm, query_ref),
                (keys_hbm, keys_ref),
                (values_hbm, values_ref),
                (hidden_hbm, hidden_ref),
            )
        )
    ]
    for copy in copies:
        copy.start()
    column = lax.broadcasted_iota(jnp.int32, (heads, slots), 1)
    owner = lax.broadcasted_iota(jnp.int32, (heads, slots), 0) // group
    position = column - owner * span
    for copy in copies[:3]:
        copy.wait()
    scores = [
        lax.dot_general(
            query_ref[r],
            keys_ref[r].reshape(slots, head_size),
            (((1,), (1,)), ((), ())),
            preferred_element_type=jnp.float32,
        )
        for r in range(requests)
    ]
    probs = []
    for r in range(requests):
        visible = (position >= 0) & (position < jnp.minimum(lengths_ref[r], span))
        score = jnp.where(visible, scores[r] * head_size ** (-0.5), -1e30)
        weight = jnp.exp(score - jnp.max(score, axis=1, keepdims=True))
        probs.append((weight / jnp.sum(weight, axis=1, keepdims=True)).astype(jnp.bfloat16))
    copies[3].wait()
    for r in range(requests):
        rows_ref[r] = jnp.dot(
            probs[r], values_ref[r].reshape(slots, head_size), preferred_element_type=jnp.float32
        )
    for h in range(heads):
        value = rows_ref[:, h, :].astype(jnp.bfloat16)
        for out_ref in out_refs:
            out_ref[:, h * head_size : (h + 1) * head_size] = value
    half = hidden_ref.shape[1] // (2 * dev_count)
    copies[4].wait()
    for out_ref, peers in zip(out_refs, steps):
        for number, peer in enumerate(peers):
            at = pl.multiple_of(((me ^ peer) * 2 + sub) * half, LANES)
            to = heads * head_size + number * half
            out_ref[:, to : to + half] = hidden_ref[:, pl.ds(at, half)]


def half_block(piece, width):
    sub = lax.axis_index("sub")
    side = sub if piece[1] else 1 - sub
    return pl.multiple_of(((lax.axis_index("dev") ^ piece[0]) * 2 + side) * width, LANES)


def weight_copies(piece, sources, targets, sems):
    width, units = targets[0].shape
    at = pl.ds(half_block(piece, width), width)
    part = units // COLUMN_PARTS
    return [
        pltpu.make_async_copy(
            source.at[at, k * part : (k + 1) * part],
            target.at[:, k * part : (k + 1) * part],
            sems.at[number * COLUMN_PARTS + k],
        )
        for number, (source, target) in enumerate(zip(sources, targets))
        for k in range(COLUMN_PARTS)
    ]


def prefetch_kernel(pieces, plain, after_ref, *refs):
    sources, outputs, sems, plain_sems = refs[: 2 + plain], refs[2 + plain : -2], refs[-2], refs[-1]
    copies = [
        pltpu.make_async_copy(source, target, plain_sems.at[number])
        for number, (source, target) in enumerate(zip(sources[2:], outputs[2:]))
    ]
    for index, piece in enumerate(pieces):
        copies += weight_copies(piece, sources[:2], [ref.at[index] for ref in outputs[:2]], sems.at[index])
    for copy in copies:
        copy.start()
    for copy in copies:
        copy.wait()


def join_kernel(width, *refs):
    out_ref, at = refs[-1], 0
    for ref in refs[:-1]:
        out_ref[at : at + ref.shape[0]] = ref[...] if width is None else ref[:, :width]
        at += ref.shape[0]


def projection_kernel(origins, weight_ref, *refs):
    got_refs, (out_ref, stacked) = refs[:-2], refs[-2:]
    me, sub = lax.axis_index("dev"), lax.axis_index("sub")
    own_rows = out_ref.shape[0] // len(origins)
    depth = weight_ref.shape[0]
    half = out_ref.shape[1] // 2
    for number, (operand, row, _, _) in enumerate(origins):
        stacked[number * own_rows : (number + 1) * own_rows, :] = got_refs[operand][row : row + own_rows, :depth]
    product = jnp.dot(stacked[...], weight_ref[...], preferred_element_type=jnp.float32)
    columns = pl.ds(pl.multiple_of(sub * half, LANES), half)
    for number, (operand, row, column, owner) in enumerate(origins):
        rows = pl.ds(pl.multiple_of((me ^ owner) * own_rows, own_rows), own_rows)
        piece = got_refs[operand][row : row + own_rows, column : column + half].astype(jnp.float32)
        out_ref[rows, :] = product[number * own_rows : (number + 1) * own_rows, :]
        out_ref[rows, columns] = out_ref[rows, columns] + piece


def residual_kernel(mine_ref, other_ref, full_ref, half_ref, sums):
    sub = lax.axis_index("sub")
    half = half_ref.shape[1]
    sums[...] = mine_ref[...] + other_ref[...]
    full_ref[...] = sums[...].astype(jnp.bfloat16)
    half_ref[...] = sums[:, pl.ds(pl.multiple_of(sub * half, LANES), half)].astype(jnp.bfloat16)


def expert_in_kernel(plan, places, groups, width, first, last, *refs):
    refs = list(refs)

    def take(count):
        taken, refs[:] = refs[:count], refs[count:]
        return taken

    operands = 1 + max(piece[0] for piece in plan)
    sources = take(2)
    held = [take(2) for _ in range(groups)]
    mine_ref, theirs_ref, router_ref, gain_ref = take(4)
    x_refs = take(operands)
    before = None if first else take(4)
    if last:
        *last_sources, down_ref = take(4)
        inner_ref, share_ref, resid_ref, fetched_ref = take(4)
    else:
        gate_sum, up_sum, small, resid_ref = take(4)
    streamed = [piece[2] for piece, place in zip(plan, places) if place is None]
    copies = []
    if streamed:
        gate_buf, up_buf, sems = take(3)
        copies = [
            weight_copies(piece, sources, [gate_buf.at[slot], up_buf.at[slot]], sems.at[slot])
            for slot, piece in enumerate(streamed)
        ]
        for copy in sum(copies, []):
            copy.start()
    if last:
        gate_sum, up_sum, small, names, gate_low_ref, up_low_ref, last_sems = take(7)
        last_copies = [
            pltpu.make_async_copy(source, target, last_sems.at[number])
            for number, (source, target) in enumerate(zip(last_sources, (names, gate_low_ref, up_low_ref)))
        ]
        last_copies.append(down_copy(down_ref, False, 0, fetched_ref, last_sems.at[3]))
        for copy in last_copies:
            copy.start()
    me, sub = lax.axis_index("dev"), lax.axis_index("sub")
    rank, experts = mine_ref.shape[1], router_ref.shape[0]
    factor_rows = mine_ref.shape[0]
    own_rows, model_width = resid_ref.shape
    if first:
        gate_sum[...] = jnp.zeros_like(gate_sum)
        up_sum[...] = jnp.zeros_like(up_sum)
        small[...] = jnp.zeros_like(small)
    else:
        for now, earlier in zip((gate_sum, up_sum, small, resid_ref), before):
            now[...] = earlier[...]
    my_rows = pl.ds(pl.multiple_of(me * own_rows, own_rows), own_rows)
    slot = 0
    for (operand, which, piece), place in zip(plan, places):
        base = half_block(piece, width)
        if which is None:
            side = sub if piece[1] else 1 - sub
            source, columns = x_refs[operand], pl.ds(pl.multiple_of(side * width, LANES), width)
        else:
            source, columns = x_refs[operand].at[which], slice(0, width)
        x = source[:, columns].astype(jnp.float32)
        small[:, rank + LANES :] += jnp.sum(x * x, axis=1, keepdims=True)
        resid_ref[:, pl.ds(base, width)] = source[my_rows, columns]
        x = (x * gain_ref[:, pl.ds(base, width)]).astype(jnp.bfloat16)
        small[:, rank : rank + experts] += lax.dot_general(
            x, router_ref[:, pl.ds(base, width)], (((1,), (1,)), ((), ())), preferred_element_type=jnp.float32
        )
        if place is None:
            gate_ref, up_ref, index = gate_buf, up_buf, slot
            for copy in copies[slot]:
                copy.wait()
            slot += 1
        else:
            (gate_ref, up_ref), index = held[place[0]], place[1]
        upper = base >= factor_rows
        at = pl.ds(pl.multiple_of(jnp.where(upper, base - factor_rows, base), LANES), width)
        factor = jnp.where(upper == (sub == 1), mine_ref[at, :], theirs_ref[at, :])
        small[:, :rank] += jnp.dot(x, factor, preferred_element_type=jnp.float32)
        gate_sum[...] += jnp.dot(x, gate_ref[index], preferred_element_type=jnp.float32)
        up_sum[...] += jnp.dot(x, up_ref[index], preferred_element_type=jnp.float32)
    if not last:
        return
    for copy in last_copies[:3]:
        copy.wait()
    inverse = lax.rsqrt(small[:, rank + LANES : rank + LANES + 1] / model_width + EPSILON)
    low_rank = (small[:, :rank] * inverse).astype(jnp.bfloat16)
    gate = gate_sum[...] * inverse + jnp.dot(
        low_rank, gate_low_ref[...], preferred_element_type=jnp.float32
    )
    up = up_sum[...] * inverse + jnp.dot(
        low_rank, up_low_ref[...], preferred_element_type=jnp.float32
    )
    inner_ref[...] = (jax.nn.silu(gate) * up).astype(jnp.bfloat16)
    mine = small[my_rows, :]
    inverse = lax.rsqrt(mine[:, rank + LANES : rank + LANES + 1] / model_width + EPSILON)
    logits = mine[:, rank : rank + LANES] * inverse
    lanes = lax.broadcasted_iota(jnp.int32, (own_rows, LANES), 1)
    numbers = lax.broadcasted_iota(jnp.int32, (own_rows, LANES), 0)
    one, two = jnp.zeros_like(numbers), jnp.zeros_like(numbers)
    for r in range(own_rows):
        one = jnp.where(numbers == r, names[0, r], one)
        two = jnp.where(numbers == r, names[1, r], two)
    chosen_one = jnp.sum(jnp.where(lanes == one, logits, 0.0), axis=1, keepdims=True)
    chosen_two = jnp.sum(jnp.where(lanes == two, logits, 0.0), axis=1, keepdims=True)
    leading = jax.nn.sigmoid(chosen_one - chosen_two)
    share_ref[...] = jnp.where(lanes == one, leading, 0.0) + jnp.where(lanes == two, 1.0 - leading, 0.0)
    last_copies[3].wait()


def down_copy(down_ref, own, first, target, sem):
    rows, columns = target.shape
    sub = lax.axis_index("sub")
    start = pl.multiple_of((sub if own else 1 - sub) * columns, LANES)
    return pltpu.make_async_copy(down_ref.at[first : first + rows, pl.ds(start, columns)], target, sem)


def expert_out_kernel(own, down_ref, inner_ref, ready_ref, out_ref, *refs):
    sums, buf, sems = refs[-3:]
    blocks, block, _ = buf.shape
    ready = ready_ref.shape[0]
    copies = [
        down_copy(down_ref, own, ready + index * block, buf.at[index], sems.at[index]) for index in range(blocks)
    ]
    if not own:
        copies.append(down_copy(down_ref, True, 0, refs[0], sems.at[blocks]))
    for copy in copies:
        copy.start()
    sums[...] = jnp.dot(inner_ref[:, :ready], ready_ref[...], preferred_element_type=jnp.float32)
    for index in range(blocks):
        copies[index].wait()
        at = ready + index * block
        sums[...] += jnp.dot(inner_ref[:, at : at + block], buf[index], preferred_element_type=jnp.float32)
    out_ref[...] = sums[...].astype(out_ref.dtype)
    if not own:
        copies[blocks].wait()


def split_kernel(mine_ref, other_ref, out_ref):
    peers, rows, _ = out_ref.shape
    for peer in range(peers):
        at = slice(peer * rows, (peer + 1) * rows)
        out_ref[peer] = (mine_ref[at, :] + other_ref[at, :].astype(jnp.float32)).astype(jnp.bfloat16)


def mixture_kernel(holders, share_ref, parts_ref, out_ref):
    total = jnp.zeros(out_ref.shape, jnp.float32)
    for expert in range(parts_ref.shape[0] // holders):
        held = parts_ref[expert * holders].astype(jnp.float32)
        for holder in range(1, holders):
            held = held + parts_ref[expert * holders + holder].astype(jnp.float32)
        total = total + held * share_ref[:, expert : expert + 1]
    out_ref[...] = total.astype(jnp.bfloat16)


def output_kernel(mine_ref, other_ref, resid_ref, layer_ref, mixture_ref):
    sub = lax.axis_index("sub")
    half = mine_ref.shape[1]
    for ref, side in ((mine_ref, sub), (other_ref, 1 - sub)):
        at = pl.ds(pl.multiple_of(side * half, LANES), half)
        mixture = ref[...].astype(jnp.float32)
        mixture_ref[:, at] = mixture
        layer_ref[:, at] = (resid_ref[:, at].astype(jnp.float32) + mixture).astype(jnp.bfloat16)


def fast_body(
    hidden,
    query,
    cache_keys,
    cache_values,
    lengths,
    out_proj,
    norm_gain,
    router,
    low_factor,
    gate_weight,
    up_weight,
    down_weight,
    gate_low,
    up_low,
    experts,
):
    dev_count = lax.axis_size("dev")
    holders = dev_count // router.shape[1]
    own_rows, model_width = hidden.shape
    rows = own_rows * dev_count
    width = model_width // dev_count
    half = width // 2
    units = gate_weight.shape[1]
    rank = low_factor.shape[1]
    heads_width = query.shape[1] * query.shape[2]
    bf16, f32 = jnp.bfloat16, jnp.float32
    shape = jax.ShapeDtypeStruct

    def across(value, step):
        return lax.ppermute(value, "dev", [(i, i ^ step) for i in range(dev_count)])

    def other_core(value):
        return lax.ppermute(value, "sub", [(0, 1), (1, 0)])

    def join(values, columns=None):
        kind = values[0].shape[1:] if columns is None else (columns,)
        return pl.pallas_call(
            functools.partial(join_kernel, columns),
            out_shape=shape((sum(value.shape[0] for value in values),) + kind, bf16),
            in_specs=[vmem()] * len(values),
            out_specs=vmem(),
            compiler_params=params(2),
            name="join",
        )(*values)

    bits = []
    while 2 << len(bits) < dev_count:
        bits.insert(0, 2 << len(bits))
    seen, paired, plans = [0], [], [[(0, None, (0, True)), (0, None, (0, False))]]
    stages = []
    fresh, late = [0], []
    for bit in bits + [None]:
        arrived = [] if bit is None else [owner ^ bit for owner in seen]
        turned = [owner ^ 1 for owner in fresh]
        stages.append((bit, arrived, turned))
        early = [(0, k, (owner, True)) for k, owner in enumerate(arrived + turned)]
        plans.append(late + early)
        late = [(1, k, (owner, False)) for k, owner in enumerate(arrived + turned)]
        seen, fresh = seen + arrived, arrived
    plans.append([(0,) + piece[1:] for piece in late])

    ready = [piece[2] for plan, count in zip(plans, READY) for piece in plan[:count]]
    pieces_of = [ready[:PREFETCH_FIRST], ready[PREFETCH_FIRST:]]
    where = {piece: (group, index) for group in range(2) for index, piece in enumerate(pieces_of[group])}

    theirs = other_core(low_factor)
    sources = [in_hbm(gate_weight), in_hbm(up_weight)]

    upper = list(range(2, dev_count, 2))
    steps = [(0,), (1,)] + [(step ^ 1, step) for step in upper]
    sent = pl.pallas_call(
        functools.partial(attention_kernel, dev_count, steps),
        out_shape=[shape((own_rows, heads_width + half * len(peers)), bf16) for peers in steps],
        in_specs=[hbm()] * 5,
        out_specs=[vmem()] * len(steps),
        scratch_shapes=[
            pltpu.SMEM(lengths.shape, jnp.int32),
            pltpu.VMEM(query.shape, bf16),
            pltpu.VMEM(cache_keys.shape, bf16),
            pltpu.VMEM(cache_values.shape, bf16),
            pltpu.VMEM(hidden.shape, bf16),
            pltpu.VMEM(query.shape, f32),
            pltpu.SemaphoreType.DMA((5,)),
        ],
        compiler_params=params(8),
        name="attention",
    )(*map(in_hbm, (lengths, query, cache_keys, cache_values, hidden)))

    def prefetch(group, after, plain):
        pieces = pieces_of[group]
        return pl.pallas_call(
            functools.partial(prefetch_kernel, pieces, len(plain)),
            out_shape=[shape((len(pieces), half, units), bf16)] * 2
            + [shape(value.shape, value.dtype) for value in plain],
            in_specs=[vmem()] + [hbm()] * (2 + len(plain)),
            out_specs=[vmem()] * (2 + len(plain)),
            scratch_shapes=[pltpu.SemaphoreType.DMA((len(pieces), 2 * COLUMN_PARTS)), pltpu.SemaphoreType.DMA((max(1, len(plain)),))],
            compiler_params=params(2),
            cost_estimate=cost(0, 4 * len(pieces) * half * units),
            name="prefetch_%d" % group,
        )(after, *sources, *plain)

    got = [across(sent[2 + k], step) for k, step in enumerate(upper)]
    got_pair = across(sent[1], 1)
    gain = norm_gain.reshape(1, model_width)
    fetched = prefetch(0, sent[0], [in_hbm(value) for value in (out_proj, low_factor, router.T, gain)])
    held, (projection_weight, factor, router_rows, gain) = [fetched[:2]], fetched[2:]
    got, got_pair, gain = lax.optimization_barrier((got, got_pair, gain))
    packed = join(got, heads_width + half)
    got_packed = across(packed, 1)
    held.append(prefetch(1, packed, []))
    projection_weight, held[1] = lax.optimization_barrier((projection_weight, held[1]))

    origins = [(0, 0, heads_width, 0), (1, 0, heads_width, 1)]
    origins += [(2 + k, 0, heads_width + half, step) for k, step in enumerate(upper)]
    origins += [(2 + len(upper), k * own_rows, heads_width, step ^ 1) for k, step in enumerate(upper)]
    partial_proj = pl.pallas_call(
        functools.partial(projection_kernel, origins),
        out_shape=shape((rows, width), f32),
        in_specs=[vmem()] * (4 + len(upper)),
        out_specs=vmem(),
        scratch_shapes=[pltpu.VMEM((rows, heads_width), bf16)],
        compiler_params=params(4),
        cost_estimate=cost(2 * rows * out_proj.size, 2 * out_proj.size),
        name="projection",
    )(projection_weight, sent[0], got_pair, *got, got_packed)
    full, own_half = pl.pallas_call(
        residual_kernel,
        out_shape=[shape((rows, width), bf16), shape((rows, half), bf16)],
        in_specs=[vmem()] * 2,
        out_specs=[vmem()] * 2,
        scratch_shapes=[pltpu.VMEM((rows, width), f32)],
        compiler_params=params(4),
        name="residual",
    )(partial_proj, other_core(partial_proj))

    state_shapes = [
        shape((rows, units), f32),
        shape((rows, units), f32),
        shape((rows, rank + 2 * LANES), f32),
        shape((own_rows, model_width), bf16),
    ]

    fetched_down = shape((DOWN_READY * units // 8, model_width // 2), bf16)

    def expert_in(number, operands, state, last_inputs=None):
        plan = plans[number]
        first, last = state is None, last_inputs is not None
        used = sorted({where[piece[2]][0] for piece in plan if piece[2] in where})
        places = [
            (used.index(where[piece[2]][0]), where[piece[2]][1]) if piece[2] in where else None for piece in plan
        ]
        streamed = places.count(None)
        inputs = list(sources)
        specs = [hbm()] * 2
        for number_used in used:
            inputs += held[number_used]
        inputs += [factor, theirs, router_rows, gain] + operands
        if not first:
            inputs += state
        specs += [vmem()] * (len(inputs) - len(specs))
        scratch = []
        if streamed:
            scratch += [pltpu.VMEM((streamed, half, units), bf16)] * 2 + [pltpu.SemaphoreType.DMA((streamed, 2 * COLUMN_PARTS))]
        if last:
            inputs += last_inputs
            specs += [hbm()] * 4
            out_shape = [shape((rows, units), bf16), shape((own_rows, LANES), f32), state_shapes[3], fetched_down]
            scratch += [pltpu.VMEM(kept.shape, f32) for kept in state_shapes[:3]]
            scratch += [pltpu.SMEM(experts.shape[::-1], jnp.int32)]
            scratch += [pltpu.VMEM((rank, units), bf16)] * 2 + [pltpu.SemaphoreType.DMA((4,))]
        else:
            out_shape = list(state_shapes)
        depth = len(plan) * half
        limit = 4 + 5 * last + -(-streamed * half * units * 4 // MIB)
        result = pl.pallas_call(
            functools.partial(expert_in_kernel, plan, places, len(used), half, first, last),
            out_shape=out_shape,
            in_specs=specs,
            out_specs=[vmem()] * len(out_shape),
            scratch_shapes=scratch,
            compiler_params=params(limit),
            cost_estimate=cost(4 * rows * depth * units, 4 * depth * units),
            name="expert_in_%d" % number,
        )(*inputs)
        return list(result)

    have, fresh, late, state = own_half[None], own_half[None], None, None
    for number, (bit, arrived, turned) in enumerate(stages):
        flying = [] if bit is None else [across(have, bit)]
        flying.append(across(fresh, 1))
        late_now = late
        operands = [full] if number == 0 else [new] + ([] if late_now is None else [late_now])
        state = expert_in(number, operands, state)
        if number:
            late_sent = other
        else:
            late_sent = None
        state, flying, late = lax.optimization_barrier((state, flying, late_sent))
        new = join(flying) if len(flying) > 1 else flying[0]
        other = other_core(new)
        if bit is not None:
            fresh = flying[0]
            have = join([have, fresh])
    number = len(stages)
    state = expert_in(number, [new] + ([] if late is None else [late]), state)
    state, other = lax.optimization_barrier((state, other))
    last_inputs = [in_hbm(value) for value in (experts.T, gate_low, up_low, down_weight)]
    inner, share, resid, fetched_first = expert_in(number + 1, [other], state, last_inputs)

    def expert_out(own, ready):
        out_shape = [shape((rows, model_width // 2), f32 if own else bf16)] + ([] if own else [fetched_down])
        blocks = 8 - DOWN_READY
        return pl.pallas_call(
            functools.partial(expert_out_kernel, own),
            out_shape=out_shape,
            in_specs=[hbm(), vmem(), vmem()],
            out_specs=[vmem()] * len(out_shape),
            scratch_shapes=[
                pltpu.VMEM((rows, model_width // 2), f32),
                pltpu.VMEM((blocks, units // 8, model_width // 2), bf16),
                pltpu.SemaphoreType.DMA((blocks + 1,)),
            ],
            compiler_params=params(18),
            cost_estimate=cost(rows * model_width * units, model_width * units),
            name="expert_out_own" if own else "expert_out_other",
        )(in_hbm(down_weight), inner, ready)

    to_other, fetched_first = expert_out(False, fetched_first)
    from_other = other_core(to_other)
    (own_sum,) = expert_out(True, fetched_first)
    parts = pl.pallas_call(
        split_kernel,
        out_shape=shape((dev_count, own_rows, model_width // 2), bf16),
        in_specs=[vmem()] * 2,
        out_specs=vmem(),
        compiler_params=params(4),
        name="split",
    )(own_sum, from_other)
    parts = lax.all_to_all(parts, "dev", split_axis=0, concat_axis=0, tiled=True)
    mine = pl.pallas_call(
        functools.partial(mixture_kernel, holders),
        out_shape=shape((own_rows, model_width // 2), bf16),
        in_specs=[vmem()] * 2,
        out_specs=vmem(),
        compiler_params=params(4),
        name="mixture",
    )(share, parts)
    return pl.pallas_call(
        output_kernel,
        out_shape=[shape((own_rows, model_width), bf16), shape((own_rows, model_width), f32)],
        in_specs=[vmem()] * 3,
        out_specs=[vmem()] * 2,
        compiler_params=params(4),
        name="output",
    )(mine, other_core(mine), resid)


def expert_shard(row_block, low_rank, gate_weight, up_weight, down_weight, gate_low, up_low):
    gate_sum = jnp.dot(row_block, gate_weight, preferred_element_type=jnp.float32) + jnp.dot(
        low_rank, gate_low, preferred_element_type=jnp.float32
    )
    up_sum = jnp.dot(row_block, up_weight, preferred_element_type=jnp.float32) + jnp.dot(
        low_rank, up_low, preferred_element_type=jnp.float32
    )
    inner_act = (jax.nn.silu(gate_sum) * up_sum).astype(jnp.bfloat16)
    return jnp.dot(inner_act, down_weight, preferred_element_type=jnp.float32)


def route_gates(normed, router, experts):
    logits = jnp.dot(normed, router, preferred_element_type=jnp.float32)
    labels = lax.broadcasted_iota(jnp.int32, (1, 1, router.shape[1]), 2)
    picked = (experts[:, :, None] == labels).astype(jnp.float32)
    chosen = jnp.sum(logits[:, None, :] * picked, axis=-1)
    leading = jax.nn.sigmoid(chosen[:, 0] - chosen[:, 1])
    return jnp.stack([leading, 1.0 - leading], axis=-1)


def general_body(
    hidden,
    query,
    cache_keys,
    cache_values,
    lengths,
    out_proj,
    norm_gain,
    router,
    low_factor,
    gate_weight,
    up_weight,
    down_weight,
    gate_low,
    up_low,
    experts,
):
    requests = hidden.shape[0]
    model_width = hidden.shape[1]
    heads_here = query.shape[1]
    kv_here = cache_keys.shape[1]
    span_len = cache_keys.shape[2]
    head_size = query.shape[2]
    grouped = query.reshape(requests, kv_here, heads_here // kv_here, head_size)
    scores = jnp.einsum(
        "rkgd,rkld->rkgl", grouped, cache_keys, preferred_element_type=jnp.float32
    ) * head_size ** (-0.5)
    visible = lax.broadcasted_iota(jnp.int32, (requests, span_len), 1) < lengths[:, None]
    scores = jnp.where(visible[:, None, None, :], scores, -1e30)
    attn_probs = jax.nn.softmax(scores, axis=-1).astype(jnp.bfloat16)
    attended = jnp.einsum(
        "rkgl,rkld->rkgd", attn_probs, cache_values, preferred_element_type=jnp.float32
    )
    attended = attended.astype(jnp.bfloat16).reshape(requests, heads_here * head_size)
    columns = jnp.dot(
        lax.all_gather(attended, "dev", axis=0, tiled=True),
        out_proj,
        preferred_element_type=jnp.float32,
    )
    partial_proj = lax.all_to_all(columns, "dev", split_axis=0, concat_axis=1, tiled=True)
    residual = hidden.astype(jnp.float32) + lax.psum(partial_proj, "sub")
    inverse = lax.rsqrt(jnp.mean(residual * residual, axis=-1, keepdims=True) + EPSILON)
    normed = (residual * inverse * norm_gain).astype(jnp.bfloat16)
    half_width = low_factor.shape[0]
    normed_half = lax.dynamic_slice_in_dim(
        normed, lax.axis_index("sub") * half_width, half_width, 1
    )
    low_partial = jnp.dot(normed_half, low_factor, preferred_element_type=jnp.float32)
    low_rank = lax.psum(low_partial, "sub").astype(jnp.bfloat16)
    rank_width = low_rank.shape[1]
    expert_count = router.shape[1]
    holders = lax.axis_size("dev") // expert_count
    gate_pair = route_gates(normed, router, experts)
    flat_ids = experts.reshape(-1)
    entries = flat_ids.shape[0]
    same_expert = flat_ids[:, None] == flat_ids[None, :]
    earlier = lax.broadcasted_iota(jnp.int32, (entries, entries), 0) > lax.broadcasted_iota(
        jnp.int32, (entries, entries), 1
    )
    slot_index = jnp.sum((same_expert & earlier).astype(jnp.int32), axis=1).reshape(requests, 2)
    target = experts * CAP + slot_index
    placement = (
        target[:, :, None] == lax.broadcasted_iota(jnp.int32, (1, 1, expert_count * CAP), 2)
    ).astype(jnp.float32)
    chosen = jnp.sum(placement, axis=1).astype(jnp.bfloat16)
    packed_rows = jnp.einsum(
        "rs,rd->sd", chosen, normed, preferred_element_type=jnp.float32
    ).astype(jnp.bfloat16)
    packed_low = jnp.einsum(
        "rs,rd->sd", chosen, low_rank, preferred_element_type=jnp.float32
    ).astype(jnp.bfloat16)
    send_rows = jnp.repeat(packed_rows.reshape(expert_count, CAP, model_width), holders, axis=0)
    send_low = jnp.repeat(packed_low.reshape(expert_count, CAP, rank_width), holders, axis=0)
    got_rows = lax.all_to_all(send_rows, "dev", split_axis=0, concat_axis=0, tiled=True)
    got_low = lax.all_to_all(send_low, "dev", split_axis=0, concat_axis=0, tiled=True)
    sources = got_rows.shape[0]
    slot_count = got_rows.shape[1]
    result = expert_shard(
        got_rows.reshape(sources * slot_count, model_width),
        got_low.reshape(sources * slot_count, rank_width),
        gate_weight,
        up_weight,
        down_weight,
        gate_low,
        up_low,
    )
    partials = result.reshape(sources, slot_count, model_width)
    returned = lax.all_to_all(
        partials.astype(jnp.bfloat16), "dev", split_axis=0, concat_axis=0, tiled=True
    ).astype(partials.dtype)
    per_slot = jnp.sum(returned.reshape(expert_count, holders, CAP, model_width), axis=1).reshape(
        expert_count * CAP, model_width
    )
    weighted = jnp.sum(placement * gate_pair[:, :, None], axis=1)
    mixture_part = jnp.dot(weighted, per_slot, precision=lax.Precision.HIGHEST)
    mixture = lax.psum(mixture_part.astype(jnp.bfloat16), "sub").astype(jnp.float32)
    return ((residual + mixture).astype(jnp.bfloat16), mixture)


def body(*arrays):
    hidden, query, out_proj, router, units = arrays[0], arrays[1], arrays[5], arrays[7], arrays[9].shape[1]
    dev_count = lax.axis_size("dev")
    fits = (
        lax.axis_size("sub") == 2
        and dev_count >= 4
        and dev_count & (dev_count - 1) == 0
        and dev_count % router.shape[1] == 0
        and hidden.shape[0] == 8
        and hidden.shape[1] % (4 * LANES * dev_count) in (0, 2 * LANES * dev_count)
        and hidden.shape[1] * units <= 6144 * 2048
        and query.shape[2] == LANES
    )
    return (fast_body if fits else general_body)(*arrays)


def solution(mesh):
    placed = (
        P(("groups", "dev"), None),
        P(("groups", "dev"), "sub", None),
        P(("groups", "dev"), "sub", None, None),
        P(("groups", "dev"), "sub", None, None),
        P(("groups", "dev")),
        P("sub", "dev"),
        P(),
        P(),
        P("sub", None),
        P(None, ("dev", "sub")),
        P(None, ("dev", "sub")),
        P(("dev", "sub"), None),
        P(None, ("dev", "sub")),
        P(None, ("dev", "sub")),
        P(("groups", "dev"), None),
    )
    return jax.shard_map(
        body,
        mesh=mesh,
        in_specs=placed,
        out_specs=(P(("groups", "dev"), None), P(("groups", "dev"), None)),
        check_vma=False,
    )
```

```python
import functools

import jax
import jax.numpy as jnp
from jax import lax
from jax.experimental import pallas as pl
from jax.experimental.pallas import tpu as pltpu
from jax.sharding import PartitionSpec as P

CAP = 6
EPSILON = 1e-05
READY = (1,0,1,1,2)
PREFETCH_FIRST = 1
COLUMN_PARTS = 1
DOWN_READY = 4
MIB = 1 << 20
LANES = 128


def vmem():
    return pl.BlockSpec(memory_space=pltpu.VMEM)


def hbm():
    return pl.BlockSpec(memory_space=pltpu.HBM)


def in_hbm(value):
    return pltpu.with_memory_space_constraint(value, pltpu.HBM)


def params(limit_mib):
    return pltpu.CompilerParams(vmem_limit_bytes=limit_mib * MIB)


def cost(flops, bytes_accessed):
    return pl.CostEstimate(flops=int(flops), bytes_accessed=int(bytes_accessed), transcendentals=0)


def attention_kernel(
    dev_count, steps, lengths_hbm, query_hbm, keys_hbm, values_hbm, hidden_hbm, *refs
):
    out_refs, refs = refs[: len(steps)], refs[len(steps) :]
    lengths_ref, query_ref, keys_ref, values_ref, hidden_ref, rows_ref, sems = refs
    me, sub = lax.axis_index("dev"), lax.axis_index("sub")
    requests, heads, head_size = query_ref.shape
    kv_heads, span = keys_ref.shape[1], keys_ref.shape[2]
    group = heads // kv_heads
    slots = kv_heads * span
    copies = [
        pltpu.make_async_copy(source, target, sems.at[number])
        for number, (source, target) in enumerate(
            (
                (lengths_hbm, lengths_ref),
                (query_hbm, query_ref),
                (keys_hbm, keys_ref),
                (values_hbm, values_ref),
                (hidden_hbm, hidden_ref),
            )
        )
    ]
    for copy in copies:
        copy.start()
    column = lax.broadcasted_iota(jnp.int32, (heads, slots), 1)
    owner = lax.broadcasted_iota(jnp.int32, (heads, slots), 0) // group
    position = column - owner * span
    for copy in copies[:3]:
        copy.wait()
    scores = [
        lax.dot_general(
            query_ref[r],
            keys_ref[r].reshape(slots, head_size),
            (((1,), (1,)), ((), ())),
            preferred_element_type=jnp.float32,
        )
        for r in range(requests)
    ]
    probs = []
    for r in range(requests):
        visible = (position >= 0) & (position < jnp.minimum(lengths_ref[r], span))
        score = jnp.where(visible, scores[r] * head_size ** (-0.5), -1e30)
        weight = jnp.exp(score - jnp.max(score, axis=1, keepdims=True))
        probs.append((weight / jnp.sum(weight, axis=1, keepdims=True)).astype(jnp.bfloat16))
    copies[3].wait()
    for r in range(requests):
        rows_ref[r] = jnp.dot(
            probs[r], values_ref[r].reshape(slots, head_size), preferred_element_type=jnp.float32
        )
    for h in range(heads):
        value = rows_ref[:, h, :].astype(jnp.bfloat16)
        for out_ref in out_refs:
            out_ref[:, h * head_size : (h + 1) * head_size] = value
    half = hidden_ref.shape[1] // (2 * dev_count)
    copies[4].wait()
    for out_ref, peers in zip(out_refs, steps):
        for number, peer in enumerate(peers):
            at = pl.multiple_of(((me ^ peer) * 2 + sub) * half, LANES)
            to = heads * head_size + number * half
            out_ref[:, to : to + half] = hidden_ref[:, pl.ds(at, half)]


def half_block(piece, width):
    sub = lax.axis_index("sub")
    side = sub if piece[1] else 1 - sub
    return pl.multiple_of(((lax.axis_index("dev") ^ piece[0]) * 2 + side) * width, LANES)


def weight_copies(piece, sources, targets, sems):
    width, units = targets[0].shape
    at = pl.ds(half_block(piece, width), width)
    part = units // COLUMN_PARTS
    return [
        pltpu.make_async_copy(
            source.at[at, k * part : (k + 1) * part],
            target.at[:, k * part : (k + 1) * part],
            sems.at[number * COLUMN_PARTS + k],
        )
        for number, (source, target) in enumerate(zip(sources, targets))
        for k in range(COLUMN_PARTS)
    ]


def prefetch_kernel(pieces, plain, after_ref, *refs):
    sources, outputs, sems, plain_sems = refs[: 2 + plain], refs[2 + plain : -2], refs[-2], refs[-1]
    copies = [
        pltpu.make_async_copy(source, target, plain_sems.at[number])
        for number, (source, target) in enumerate(zip(sources[2:], outputs[2:]))
    ]
    for index, piece in enumerate(pieces):
        copies += weight_copies(piece, sources[:2], [ref.at[index] for ref in outputs[:2]], sems.at[index])
    for copy in copies:
        copy.start()
    for copy in copies:
        copy.wait()


def join_kernel(width, *refs):
    out_ref, at = refs[-1], 0
    for ref in refs[:-1]:
        out_ref[at : at + ref.shape[0]] = ref[...] if width is None else ref[:, :width]
        at += ref.shape[0]


def projection_kernel(origins, weight_ref, *refs):
    got_refs, (out_ref, stacked) = refs[:-2], refs[-2:]
    me, sub = lax.axis_index("dev"), lax.axis_index("sub")
    own_rows = out_ref.shape[0] // len(origins)
    depth = weight_ref.shape[0]
    half = out_ref.shape[1] // 2
    for number, (operand, row, _, _) in enumerate(origins):
        stacked[number * own_rows : (number + 1) * own_rows, :] = got_refs[operand][row : row + own_rows, :depth]
    product = jnp.dot(stacked[...], weight_ref[...], preferred_element_type=jnp.float32)
    columns = pl.ds(pl.multiple_of(sub * half, LANES), half)
    for number, (operand, row, column, owner) in enumerate(origins):
        rows = pl.ds(pl.multiple_of((me ^ owner) * own_rows, own_rows), own_rows)
        piece = got_refs[operand][row : row + own_rows, column : column + half].astype(jnp.float32)
        out_ref[rows, :] = product[number * own_rows : (number + 1) * own_rows, :]
        out_ref[rows, columns] = out_ref[rows, columns] + piece


def residual_kernel(mine_ref, other_ref, full_ref, half_ref, sums):
    sub = lax.axis_index("sub")
    half = half_ref.shape[1]
    sums[...] = mine_ref[...] + other_ref[...]
    full_ref[...] = sums[...].astype(jnp.bfloat16)
    half_ref[...] = sums[:, pl.ds(pl.multiple_of(sub * half, LANES), half)].astype(jnp.bfloat16)


def expert_in_kernel(plan, places, groups, width, first, last, *refs):
    refs = list(refs)

    def take(count):
        taken, refs[:] = refs[:count], refs[count:]
        return taken

    operands = 1 + max(piece[0] for piece in plan)
    sources = take(2)
    held = [take(2) for _ in range(groups)]
    mine_ref, theirs_ref, router_ref, gain_ref = take(4)
    x_refs = take(operands)
    before = None if first else take(4)
    if last:
        *last_sources, down_ref = take(4)
        inner_ref, share_ref, resid_ref, fetched_ref = take(4)
    else:
        gate_sum, up_sum, small, resid_ref = take(4)
    streamed = [piece[2] for piece, place in zip(plan, places) if place is None]
    copies = []
    if streamed:
        gate_buf, up_buf, sems = take(3)
        copies = [
            weight_copies(piece, sources, [gate_buf.at[slot], up_buf.at[slot]], sems.at[slot])
            for slot, piece in enumerate(streamed)
        ]
        for copy in sum(copies, []):
            copy.start()
    if last:
        gate_sum, up_sum, small, names, gate_low_ref, up_low_ref, last_sems = take(7)
        last_copies = [
            pltpu.make_async_copy(source, target, last_sems.at[number])
            for number, (source, target) in enumerate(zip(last_sources, (names, gate_low_ref, up_low_ref)))
        ]
        last_copies.append(down_copy(down_ref, False, 0, fetched_ref, last_sems.at[3]))
        for copy in last_copies:
            copy.start()
    me, sub = lax.axis_index("dev"), lax.axis_index("sub")
    rank, experts = mine_ref.shape[1], router_ref.shape[0]
    factor_rows = mine_ref.shape[0]
    own_rows, model_width = resid_ref.shape
    if first:
        gate_sum[...] = jnp.zeros_like(gate_sum)
        up_sum[...] = jnp.zeros_like(up_sum)
        small[...] = jnp.zeros_like(small)
    else:
        for now, earlier in zip((gate_sum, up_sum, small, resid_ref), before):
            now[...] = earlier[...]
    my_rows = pl.ds(pl.multiple_of(me * own_rows, own_rows), own_rows)
    slot = 0
    for (operand, which, piece), place in zip(plan, places):
        base = half_block(piece, width)
        if which is None:
            side = sub if piece[1] else 1 - sub
            source, columns = x_refs[operand], pl.ds(pl.multiple_of(side * width, LANES), width)
        else:
            source, columns = x_refs[operand].at[which], slice(0, width)
        x = source[:, columns].astype(jnp.float32)
        small[:, rank + LANES :] += jnp.sum(x * x, axis=1, keepdims=True)
        resid_ref[:, pl.ds(base, width)] = source[my_rows, columns]
        x = (x * gain_ref[:, pl.ds(base, width)]).astype(jnp.bfloat16)
        small[:, rank : rank + experts] += lax.dot_general(
            x, router_ref[:, pl.ds(base, width)], (((1,), (1,)), ((), ())), preferred_element_type=jnp.float32
        )
        if place is None:
            gate_ref, up_ref, index = gate_buf, up_buf, slot
            for copy in copies[slot]:
                copy.wait()
            slot += 1
        else:
            (gate_ref, up_ref), index = held[place[0]], place[1]
        upper = base >= factor_rows
        at = pl.ds(pl.multiple_of(jnp.where(upper, base - factor_rows, base), LANES), width)
        factor = jnp.where(upper == (sub == 1), mine_ref[at, :], theirs_ref[at, :])
        small[:, :rank] += jnp.dot(x, factor, preferred_element_type=jnp.float32)
        gate_sum[...] += jnp.dot(x, gate_ref[index], preferred_element_type=jnp.float32)
        up_sum[...] += jnp.dot(x, up_ref[index], preferred_element_type=jnp.float32)
    if not last:
        return
    for copy in last_copies[:3]:
        copy.wait()
    inverse = lax.rsqrt(small[:, rank + LANES : rank + LANES + 1] / model_width + EPSILON)
    low_rank = (small[:, :rank] * inverse).astype(jnp.bfloat16)
    gate = gate_sum[...] * inverse + jnp.dot(
        low_rank, gate_low_ref[...], preferred_element_type=jnp.float32
    )
    up = up_sum[...] * inverse + jnp.dot(
        low_rank, up_low_ref[...], preferred_element_type=jnp.float32
    )
    inner_ref[...] = (jax.nn.silu(gate) * up).astype(jnp.bfloat16)
    mine = small[my_rows, :]
    inverse = lax.rsqrt(mine[:, rank + LANES : rank + LANES + 1] / model_width + EPSILON)
    logits = mine[:, rank : rank + LANES] * inverse
    lanes = lax.broadcasted_iota(jnp.int32, (own_rows, LANES), 1)
    numbers = lax.broadcasted_iota(jnp.int32, (own_rows, LANES), 0)
    one, two = jnp.zeros_like(numbers), jnp.zeros_like(numbers)
    for r in range(own_rows):
        one = jnp.where(numbers == r, names[0, r], one)
        two = jnp.where(numbers == r, names[1, r], two)
    chosen_one = jnp.sum(jnp.where(lanes == one, logits, 0.0), axis=1, keepdims=True)
    chosen_two = jnp.sum(jnp.where(lanes == two, logits, 0.0), axis=1, keepdims=True)
    leading = jax.nn.sigmoid(chosen_one - chosen_two)
    share_ref[...] = jnp.where(lanes == one, leading, 0.0) + jnp.where(lanes == two, 1.0 - leading, 0.0)
    last_copies[3].wait()


def down_copy(down_ref, own, first, target, sem):
    rows, columns = target.shape
    sub = lax.axis_index("sub")
    start = pl.multiple_of((sub if own else 1 - sub) * columns, LANES)
    return pltpu.make_async_copy(down_ref.at[first : first + rows, pl.ds(start, columns)], target, sem)


def expert_out_kernel(own, down_ref, inner_ref, ready_ref, out_ref, *refs):
    sums, buf, sems = refs[-3:]
    blocks, block, _ = buf.shape
    ready = ready_ref.shape[0]
    copies = [
        down_copy(down_ref, own, ready + index * block, buf.at[index], sems.at[index]) for index in range(blocks)
    ]
    if not own:
        copies.append(down_copy(down_ref, True, 0, refs[0], sems.at[blocks]))
    for copy in copies:
        copy.start()
    sums[...] = jnp.dot(inner_ref[:, :ready], ready_ref[...], preferred_element_type=jnp.float32)
    for index in range(blocks):
        copies[index].wait()
        at = ready + index * block
        sums[...] += jnp.dot(inner_ref[:, at : at + block], buf[index], preferred_element_type=jnp.float32)
    out_ref[...] = sums[...].astype(out_ref.dtype)
    if not own:
        copies[blocks].wait()


def split_kernel(mine_ref, other_ref, out_ref):
    peers, rows, _ = out_ref.shape
    for peer in range(peers):
        at = slice(peer * rows, (peer + 1) * rows)
        out_ref[peer] = (mine_ref[at, :] + other_ref[at, :].astype(jnp.float32)).astype(jnp.bfloat16)


def mixture_kernel(holders, share_ref, parts_ref, out_ref):
    total = jnp.zeros(out_ref.shape, jnp.float32)
    for expert in range(parts_ref.shape[0] // holders):
        held = parts_ref[expert * holders].astype(jnp.float32)
        for holder in range(1, holders):
            held = held + parts_ref[expert * holders + holder].astype(jnp.float32)
        total = total + held * share_ref[:, expert : expert + 1]
    out_ref[...] = total.astype(jnp.bfloat16)


def output_kernel(mine_ref, other_ref, resid_ref, layer_ref, mixture_ref):
    sub = lax.axis_index("sub")
    half = mine_ref.shape[1]
    for ref, side in ((mine_ref, sub), (other_ref, 1 - sub)):
        at = pl.ds(pl.multiple_of(side * half, LANES), half)
        mixture = ref[...].astype(jnp.float32)
        mixture_ref[:, at] = mixture
        layer_ref[:, at] = (resid_ref[:, at].astype(jnp.float32) + mixture).astype(jnp.bfloat16)


def fast_body(
    hidden,
    query,
    cache_keys,
    cache_values,
    lengths,
    out_proj,
    norm_gain,
    router,
    low_factor,
    gate_weight,
    up_weight,
    down_weight,
    gate_low,
    up_low,
    experts,
):
    dev_count = lax.axis_size("dev")
    holders = dev_count // router.shape[1]
    own_rows, model_width = hidden.shape
    rows = own_rows * dev_count
    width = model_width // dev_count
    half = width // 2
    units = gate_weight.shape[1]
    rank = low_factor.shape[1]
    heads_width = query.shape[1] * query.shape[2]
    bf16, f32 = jnp.bfloat16, jnp.float32
    shape = jax.ShapeDtypeStruct

    def across(value, step):
        return lax.ppermute(value, "dev", [(i, i ^ step) for i in range(dev_count)])

    def other_core(value):
        return lax.ppermute(value, "sub", [(0, 1), (1, 0)])

    def join(values, columns=None):
        kind = values[0].shape[1:] if columns is None else (columns,)
        return pl.pallas_call(
            functools.partial(join_kernel, columns),
            out_shape=shape((sum(value.shape[0] for value in values),) + kind, bf16),
            in_specs=[vmem()] * len(values),
            out_specs=vmem(),
            compiler_params=params(2),
            name="join",
        )(*values)

    bits = []
    while 2 << len(bits) < dev_count:
        bits.insert(0, 2 << len(bits))
    seen, paired, plans = [0], [], [[(0, None, (0, True)), (0, None, (0, False))]]
    stages = []
    fresh, late = [0], []
    for bit in bits + [None]:
        arrived = [] if bit is None else [owner ^ bit for owner in seen]
        turned = [owner ^ 1 for owner in fresh]
        stages.append((bit, arrived, turned))
        early = [(0, k, (owner, True)) for k, owner in enumerate(arrived + turned)]
        plans.append(late + early)
        late = [(1, k, (owner, False)) for k, owner in enumerate(arrived + turned)]
        seen, fresh = seen + arrived, arrived
    plans.append([(0,) + piece[1:] for piece in late])

    ready = [piece[2] for plan, count in zip(plans, READY) for piece in plan[:count]]
    pieces_of = [ready[:PREFETCH_FIRST], ready[PREFETCH_FIRST:]]
    where = {piece: (group, index) for group in range(2) for index, piece in enumerate(pieces_of[group])}

    sources = [in_hbm(gate_weight), in_hbm(up_weight)]

    upper = list(range(dev_count - 2, 0, -2))
    steps = [(0,), (1,)] + [(step ^ 1, step) for step in upper]
    sent = pl.pallas_call(
        functools.partial(attention_kernel, dev_count, steps),
        out_shape=[shape((own_rows, heads_width + half * len(peers)), bf16) for peers in steps],
        in_specs=[hbm()] * 5,
        out_specs=[vmem()] * len(steps),
        scratch_shapes=[
            pltpu.SMEM(lengths.shape, jnp.int32),
            pltpu.VMEM(query.shape, bf16),
            pltpu.VMEM(cache_keys.shape, bf16),
            pltpu.VMEM(cache_values.shape, bf16),
            pltpu.VMEM(hidden.shape, bf16),
            pltpu.VMEM(query.shape, f32),
            pltpu.SemaphoreType.DMA((5,)),
        ],
        compiler_params=params(8),
        name="attention",
    )(*map(in_hbm, (lengths, query, cache_keys, cache_values, hidden)))

    def prefetch(group, after, plain):
        pieces = pieces_of[group]
        return pl.pallas_call(
            functools.partial(prefetch_kernel, pieces, len(plain)),
            out_shape=[shape((len(pieces), half, units), bf16)] * 2
            + [shape(value.shape, value.dtype) for value in plain],
            in_specs=[vmem()] + [hbm()] * (2 + len(plain)),
            out_specs=[vmem()] * (2 + len(plain)),
            scratch_shapes=[pltpu.SemaphoreType.DMA((len(pieces), 2 * COLUMN_PARTS)), pltpu.SemaphoreType.DMA((max(1, len(plain)),))],
            compiler_params=params(2),
            cost_estimate=cost(0, 4 * len(pieces) * half * units),
            name="prefetch_%d" % group,
        )(after, *sources, *plain)

    sent = list(sent)
    tied, sent[0] = lax.optimization_barrier((low_factor, sent[0]))
    theirs = other_core(tied)
    got = [across(sent[2 + k], step) for k, step in enumerate(upper)]
    got_pair = across(sent[1], 1)
    gain = norm_gain.reshape(1, model_width)
    fetched = prefetch(0, sent[0], [in_hbm(value) for value in (out_proj, low_factor, router.T, gain)])
    held, (projection_weight, factor, router_rows, gain) = [fetched[:2]], fetched[2:]
    got, got_pair, gain = lax.optimization_barrier((got, got_pair, gain))
    packed = join(got, heads_width + half)
    got_packed = across(packed, 1)
    held.append(prefetch(1, packed, []))
    projection_weight, held[1] = lax.optimization_barrier((projection_weight, held[1]))

    origins = [(0, 0, heads_width, 0), (1, 0, heads_width, 1)]
    origins += [(2 + k, 0, heads_width + half, step) for k, step in enumerate(upper)]
    origins += [(2 + len(upper), k * own_rows, heads_width, step ^ 1) for k, step in enumerate(upper)]
    partial_proj = pl.pallas_call(
        functools.partial(projection_kernel, origins),
        out_shape=shape((rows, width), f32),
        in_specs=[vmem()] * (4 + len(upper)),
        out_specs=vmem(),
        scratch_shapes=[pltpu.VMEM((rows, heads_width), bf16)],
        compiler_params=params(4),
        cost_estimate=cost(2 * rows * out_proj.size, 2 * out_proj.size),
        name="projection",
    )(projection_weight, sent[0], got_pair, *got, got_packed)
    full, own_half = pl.pallas_call(
        residual_kernel,
        out_shape=[shape((rows, width), bf16), shape((rows, half), bf16)],
        in_specs=[vmem()] * 2,
        out_specs=[vmem()] * 2,
        scratch_shapes=[pltpu.VMEM((rows, width), f32)],
        compiler_params=params(4),
        name="residual",
    )(partial_proj, other_core(partial_proj))

    state_shapes = [
        shape((rows, units), f32),
        shape((rows, units), f32),
        shape((rows, rank + 2 * LANES), f32),
        shape((own_rows, model_width), bf16),
    ]

    fetched_down = shape((DOWN_READY * units // 8, model_width // 2), bf16)

    def expert_in(number, operands, state, last_inputs=None):
        plan = plans[number]
        first, last = state is None, last_inputs is not None
        used = sorted({where[piece[2]][0] for piece in plan if piece[2] in where})
        places = [
            (used.index(where[piece[2]][0]), where[piece[2]][1]) if piece[2] in where else None for piece in plan
        ]
        streamed = places.count(None)
        inputs = list(sources)
        specs = [hbm()] * 2
        for number_used in used:
            inputs += held[number_used]
        inputs += [factor, theirs, router_rows, gain] + operands
        if not first:
            inputs += state
        specs += [vmem()] * (len(inputs) - len(specs))
        scratch = []
        if streamed:
            scratch += [pltpu.VMEM((streamed, half, units), bf16)] * 2 + [pltpu.SemaphoreType.DMA((streamed, 2 * COLUMN_PARTS))]
        if last:
            inputs += last_inputs
            specs += [hbm()] * 4
            out_shape = [shape((rows, units), bf16), shape((own_rows, LANES), f32), state_shapes[3], fetched_down]
            scratch += [pltpu.VMEM(kept.shape, f32) for kept in state_shapes[:3]]
            scratch += [pltpu.SMEM(experts.shape[::-1], jnp.int32)]
            scratch += [pltpu.VMEM((rank, units), bf16)] * 2 + [pltpu.SemaphoreType.DMA((4,))]
        else:
            out_shape = list(state_shapes)
        depth = len(plan) * half
        limit = 4 + 5 * last + -(-streamed * half * units * 4 // MIB)
        result = pl.pallas_call(
            functools.partial(expert_in_kernel, plan, places, len(used), half, first, last),
            out_shape=out_shape,
            in_specs=specs,
            out_specs=[vmem()] * len(out_shape),
            scratch_shapes=scratch,
            compiler_params=params(limit),
            cost_estimate=cost(4 * rows * depth * units, 4 * depth * units),
            name="expert_in_%d" % number,
        )(*inputs)
        return list(result)

    have, fresh, late, state = own_half[None], own_half[None], None, None
    for number, (bit, arrived, turned) in enumerate(stages):
        flying = [] if bit is None else [across(have, bit)]
        flying.append(across(fresh, 1))
        late_now = late
        operands = [full] if number == 0 else [new] + ([] if late_now is None else [late_now])
        state = expert_in(number, operands, state)
        if number:
            late_sent = other
        else:
            late_sent = None
        state, flying, late = lax.optimization_barrier((state, flying, late_sent))
        new = join(flying) if len(flying) > 1 else flying[0]
        other = other_core(new)
        if bit is not None:
            fresh = flying[0]
            have = join([have, fresh])
    number = len(stages)
    state = expert_in(number, [new] + ([] if late is None else [late]), state)
    state, other = lax.optimization_barrier((state, other))
    last_inputs = [in_hbm(value) for value in (experts.T, gate_low, up_low, down_weight)]
    inner, share, resid, fetched_first = expert_in(number + 1, [other], state, last_inputs)

    def expert_out(own, ready):
        out_shape = [shape((rows, model_width // 2), f32 if own else bf16)] + ([] if own else [fetched_down])
        blocks = 8 - DOWN_READY
        return pl.pallas_call(
            functools.partial(expert_out_kernel, own),
            out_shape=out_shape,
            in_specs=[hbm(), vmem(), vmem()],
            out_specs=[vmem()] * len(out_shape),
            scratch_shapes=[
                pltpu.VMEM((rows, model_width // 2), f32),
                pltpu.VMEM((blocks, units // 8, model_width // 2), bf16),
                pltpu.SemaphoreType.DMA((blocks + 1,)),
            ],
            compiler_params=params(18),
            cost_estimate=cost(rows * model_width * units, model_width * units),
            name="expert_out_own" if own else "expert_out_other",
        )(in_hbm(down_weight), inner, ready)

    to_other, fetched_first = expert_out(False, fetched_first)
    from_other = other_core(to_other)
    (own_sum,) = expert_out(True, fetched_first)
    parts = pl.pallas_call(
        split_kernel,
        out_shape=shape((dev_count, own_rows, model_width // 2), bf16),
        in_specs=[vmem()] * 2,
        out_specs=vmem(),
        compiler_params=params(4),
        name="split",
    )(own_sum, from_other)
    parts = lax.all_to_all(parts, "dev", split_axis=0, concat_axis=0, tiled=True)
    mine = pl.pallas_call(
        functools.partial(mixture_kernel, holders),
        out_shape=shape((own_rows, model_width // 2), bf16),
        in_specs=[vmem()] * 2,
        out_specs=vmem(),
        compiler_params=params(4),
        name="mixture",
    )(share, parts)
    return pl.pallas_call(
        output_kernel,
        out_shape=[shape((own_rows, model_width), bf16), shape((own_rows, model_width), f32)],
        in_specs=[vmem()] * 3,
        out_specs=[vmem()] * 2,
        compiler_params=params(4),
        name="output",
    )(mine, other_core(mine), resid)


def expert_shard(row_block, low_rank, gate_weight, up_weight, down_weight, gate_low, up_low):
    gate_sum = jnp.dot(row_block, gate_weight, preferred_element_type=jnp.float32) + jnp.dot(
        low_rank, gate_low, preferred_element_type=jnp.float32
    )
    up_sum = jnp.dot(row_block, up_weight, preferred_element_type=jnp.float32) + jnp.dot(
        low_rank, up_low, preferred_element_type=jnp.float32
    )
    inner_act = (jax.nn.silu(gate_sum) * up_sum).astype(jnp.bfloat16)
    return jnp.dot(inner_act, down_weight, preferred_element_type=jnp.float32)


def route_gates(normed, router, experts):
    logits = jnp.dot(normed, router, preferred_element_type=jnp.float32)
    labels = lax.broadcasted_iota(jnp.int32, (1, 1, router.shape[1]), 2)
    picked = (experts[:, :, None] == labels).astype(jnp.float32)
    chosen = jnp.sum(logits[:, None, :] * picked, axis=-1)
    leading = jax.nn.sigmoid(chosen[:, 0] - chosen[:, 1])
    return jnp.stack([leading, 1.0 - leading], axis=-1)


def general_body(
    hidden,
    query,
    cache_keys,
    cache_values,
    lengths,
    out_proj,
    norm_gain,
    router,
    low_factor,
    gate_weight,
    up_weight,
    down_weight,
    gate_low,
    up_low,
    experts,
):
    requests = hidden.shape[0]
    model_width = hidden.shape[1]
    heads_here = query.shape[1]
    kv_here = cache_keys.shape[1]
    span_len = cache_keys.shape[2]
    head_size = query.shape[2]
    grouped = query.reshape(requests, kv_here, heads_here // kv_here, head_size)
    scores = jnp.einsum(
        "rkgd,rkld->rkgl", grouped, cache_keys, preferred_element_type=jnp.float32
    ) * head_size ** (-0.5)
    visible = lax.broadcasted_iota(jnp.int32, (requests, span_len), 1) < lengths[:, None]
    scores = jnp.where(visible[:, None, None, :], scores, -1e30)
    attn_probs = jax.nn.softmax(scores, axis=-1).astype(jnp.bfloat16)
    attended = jnp.einsum(
        "rkgl,rkld->rkgd", attn_probs, cache_values, preferred_element_type=jnp.float32
    )
    attended = attended.astype(jnp.bfloat16).reshape(requests, heads_here * head_size)
    columns = jnp.dot(
        lax.all_gather(attended, "dev", axis=0, tiled=True),
        out_proj,
        preferred_element_type=jnp.float32,
    )
    partial_proj = lax.all_to_all(columns, "dev", split_axis=0, concat_axis=1, tiled=True)
    residual = hidden.astype(jnp.float32) + lax.psum(partial_proj, "sub")
    inverse = lax.rsqrt(jnp.mean(residual * residual, axis=-1, keepdims=True) + EPSILON)
    normed = (residual * inverse * norm_gain).astype(jnp.bfloat16)
    half_width = low_factor.shape[0]
    normed_half = lax.dynamic_slice_in_dim(
        normed, lax.axis_index("sub") * half_width, half_width, 1
    )
    low_partial = jnp.dot(normed_half, low_factor, preferred_element_type=jnp.float32)
    low_rank = lax.psum(low_partial, "sub").astype(jnp.bfloat16)
    rank_width = low_rank.shape[1]
    expert_count = router.shape[1]
    holders = lax.axis_size("dev") // expert_count
    gate_pair = route_gates(normed, router, experts)
    flat_ids = experts.reshape(-1)
    entries = flat_ids.shape[0]
    same_expert = flat_ids[:, None] == flat_ids[None, :]
    earlier = lax.broadcasted_iota(jnp.int32, (entries, entries), 0) > lax.broadcasted_iota(
        jnp.int32, (entries, entries), 1
    )
    slot_index = jnp.sum((same_expert & earlier).astype(jnp.int32), axis=1).reshape(requests, 2)
    target = experts * CAP + slot_index
    placement = (
        target[:, :, None] == lax.broadcasted_iota(jnp.int32, (1, 1, expert_count * CAP), 2)
    ).astype(jnp.float32)
    chosen = jnp.sum(placement, axis=1).astype(jnp.bfloat16)
    packed_rows = jnp.einsum(
        "rs,rd->sd", chosen, normed, preferred_element_type=jnp.float32
    ).astype(jnp.bfloat16)
    packed_low = jnp.einsum(
        "rs,rd->sd", chosen, low_rank, preferred_element_type=jnp.float32
    ).astype(jnp.bfloat16)
    send_rows = jnp.repeat(packed_rows.reshape(expert_count, CAP, model_width), holders, axis=0)
    send_low = jnp.repeat(packed_low.reshape(expert_count, CAP, rank_width), holders, axis=0)
    got_rows = lax.all_to_all(send_rows, "dev", split_axis=0, concat_axis=0, tiled=True)
    got_low = lax.all_to_all(send_low, "dev", split_axis=0, concat_axis=0, tiled=True)
    sources = got_rows.shape[0]
    slot_count = got_rows.shape[1]
    result = expert_shard(
        got_rows.reshape(sources * slot_count, model_width),
        got_low.reshape(sources * slot_count, rank_width),
        gate_weight,
        up_weight,
        down_weight,
        gate_low,
        up_low,
    )
    partials = result.reshape(sources, slot_count, model_width)
    returned = lax.all_to_all(
        partials.astype(jnp.bfloat16), "dev", split_axis=0, concat_axis=0, tiled=True
    ).astype(partials.dtype)
    per_slot = jnp.sum(returned.reshape(expert_count, holders, CAP, model_width), axis=1).reshape(
        expert_count * CAP, model_width
    )
    weighted = jnp.sum(placement * gate_pair[:, :, None], axis=1)
    mixture_part = jnp.dot(weighted, per_slot, precision=lax.Precision.HIGHEST)
    mixture = lax.psum(mixture_part.astype(jnp.bfloat16), "sub").astype(jnp.float32)
    return ((residual + mixture).astype(jnp.bfloat16), mixture)


def body(*arrays):
    hidden, query, out_proj, router, units = arrays[0], arrays[1], arrays[5], arrays[7], arrays[9].shape[1]
    dev_count = lax.axis_size("dev")
    fits = (
        lax.axis_size("sub") == 2
        and dev_count >= 4
        and dev_count & (dev_count - 1) == 0
        and dev_count % router.shape[1] == 0
        and hidden.shape[0] == 8
        and hidden.shape[1] % (4 * LANES * dev_count) in (0, 2 * LANES * dev_count)
        and hidden.shape[1] * units <= 6144 * 2048
        and query.shape[2] == LANES
    )
    return (fast_body if fits else general_body)(*arrays)


def solution(mesh):
    placed = (
        P(("groups", "dev"), None),
        P(("groups", "dev"), "sub", None),
        P(("groups", "dev"), "sub", None, None),
        P(("groups", "dev"), "sub", None, None),
        P(("groups", "dev")),
        P("sub", "dev"),
        P(),
        P(),
        P("sub", None),
        P(None, ("dev", "sub")),
        P(None, ("dev", "sub")),
        P(("dev", "sub"), None),
        P(None, ("dev", "sub")),
        P(None, ("dev", "sub")),
        P(("groups", "dev"), None),
    )
    return jax.shard_map(
        body,
        mesh=mesh,
        in_specs=placed,
        out_specs=(P(("groups", "dev"), None), P(("groups", "dev"), None)),
        check_vma=False,
    )
```
